256 devices in a mesh: blk: 32 (over z, y_hi, core), cls: 8 (over x, y_lo).
Axes of the slice: x: 4, y: 4 (y_hi: 2, y_lo: 2; y = y_hi * 2 + y_lo), z: 8, core: 2. Of those that a mesh axis runs over, the one named last changes fastest.
Arguments:
- features: bfloat16 [2048, 2048], P('blk'), may hold values from -6 to 6
- labels: int32 [2048], P('blk'), may hold values from 0 to 655359
- offset: int32 [1], replicated, may hold values from 0 to 524288
- other_lse: float32 [2048], replicated, may hold values from 15 to 20
- weight: bfloat16 [131072, 2048], P(('blk', 'cls'))
- accum: float32 [131072, 2048], P(('blk', 'cls')), may hold values from 0.1 to 1
Outputs:
- new_weight: bfloat16 [131072, 2048], P(('blk', 'cls'))
- new_accum: float32 [131072, 2048], P(('blk', 'cls'))
- lse: float32 [2048], P('blk')
The draws below stay inside these ranges and needn't reach their ends.
All inputs are finite; a program needn't handle non-finite values.
Results may differ from the reference program's by a relative error of at most 0.004.
Values may be sent and summed in bfloat16 or wider, within the bound.
A program may use at most 128 MiB of HBM per device.

```python
import math
import jax
import jax.numpy as jnp
from jax import lax

F = 2048
CLASSES = 131072
ALL_CLASSES = 655360
BATCH = 2048


def draw_features(key, part):
    key_base = jax.random.fold_in(key, 0)
    base = jax.random.truncated_normal(key_base, -4.0, 4.0, (BATCH, F), jnp.float32)
    return base.astype(jnp.bfloat16)


def draw_weight(key, part):
    base = jax.random.truncated_normal(key, -4.0, 4.0, (CLASSES, F), jnp.float32)
    place = (jnp.arange(CLASSES, dtype=jnp.float32) / CLASSES)[:, None]
    sigma = 1.3 * jnp.exp(place * jnp.log(3.0))
    return (base * sigma * F ** (-0.5)).astype(jnp.bfloat16)


def set_ends(values, key, least, high):
    spot = [jax.random.randint(jax.random.fold_in(key, axis), (), 0, length) for axis, length in enumerate(values.shape)]
    longest = values.shape.index(max(values.shape))
    neighbour = spot[:longest] + [(spot[longest] + 1) % values.shape[longest]] + spot[longest + 1:]
    return values.at[tuple(spot)].set(least).at[tuple(neighbour)].set(high)


def block_levels(key, dims, cuts, low, largest):
    def one(axis_at, parts):
        heights = jax.random.uniform(jax.random.fold_in(jax.random.fold_in(key, 6), axis_at), (parts,), jnp.float32, low / len(cuts), largest / len(cuts))
        return jnp.repeat(jnp.exp(heights), dims[axis_at] // parts).reshape((-1,) + (1,) * (len(dims) - axis_at - 1))

    gain = one(*cuts[0])
    for cut in cuts[1:]:
        gain = gain * one(*cut)
    return gain


def setup_inputs(seed: int = 0) -> dict:
    key_of = jax.random.split(jax.random.key(seed), 7)
    return {
        "features": draw_features(jax.random.fold_in(key_of[6], 71), 0),
        "labels": set_ends(jax.random.randint(key_of[1], (BATCH,), 0, ALL_CLASSES), jax.random.fold_in(key_of[1], 1), 0, ALL_CLASSES - 1).astype(jnp.int32),
        "offset": jax.random.randint(key_of[2], (1,), 0, ALL_CLASSES - CLASSES + 1).astype(jnp.int32),
        "other_lse": jnp.clip(jax.random.uniform(key_of[3], (BATCH,), jnp.float32, 15.0, 20.0), 15.0, 20.0),
        "weight": draw_weight(jax.random.fold_in(key_of[6], 71), 0),
        "accum": jnp.clip(jnp.exp(math.log(1.0) - 2.3025851 * jax.random.uniform(key_of[5], (CLASSES, F), jnp.float32) ** block_levels(key_of[5], (CLASSES, F), ((0, 256),), -0.2, 0.2)), 0.1, 1.0),
    }


def reference(features, labels, offset, other_lse, weight, accum):
    span = min(CLASSES, 8192)
    count = CLASSES // span
    w_blocks = weight.reshape(count, span, F)
    a_blocks = accum.reshape(count, span, F)
    starts = jnp.arange(count, dtype=jnp.int32) * span

    def logit_block(w_block):
        return lax.dot_general(features, w_block, (((1,), (1,)), ((), ())), preferred_element_type=jnp.float32)

    def stats(w_block):
        logits = logit_block(w_block)
        block_top = lax.optimization_barrier(jnp.max(logits, axis=1))
        block_total = lax.optimization_barrier(jnp.sum(jnp.exp(logits - block_top[:, None]), axis=1))
        return (block_top, block_total)
    tops, totals = lax.map(stats, w_blocks)
    top = lax.optimization_barrier(jnp.max(tops, axis=0))
    total = lax.optimization_barrier(jnp.sum(totals * jnp.exp(tops - top[None, :]), axis=0))
    slab_lse = top + jnp.log(total)
    high = jnp.maximum(slab_lse, other_lse)
    lse = high + jnp.log(jnp.exp(slab_lse - high) + jnp.exp(other_lse - high))

    def update(items):
        w_block, a_block, start = items
        logits = logit_block(w_block)
        local = (labels - offset[0] - start).astype(jnp.int32)
        onehot = (local[:, None] == jnp.arange(span, dtype=jnp.int32)[None, :]).astype(jnp.float32)
        delta = (jnp.exp(logits - lse[:, None]) - onehot).astype(jnp.bfloat16)
        grad = lax.dot_general(delta, features, (((0,), (0,)), ((), ())), preferred_element_type=jnp.float32)
        acc_next = a_block + grad * grad
        w_next = (w_block.astype(jnp.float32) - 0.05 * grad / (jnp.sqrt(acc_next) + 1e-10)).astype(jnp.bfloat16)
        return (w_next, acc_next)
    w_new, a_new = lax.map(update, (w_blocks, a_blocks, starts))
    return (w_new.reshape(CLASSES, F), a_new.reshape(CLASSES, F), lse)
```

```python
import functools

import jax
import jax.numpy as jnp
from jax import lax
from jax.experimental import pallas as pl
from jax.experimental.pallas import tpu as pltpu
from jax.sharding import PartitionSpec as P

MESH = pl.DeviceIdType.MESH
X, Y, Z = 4, 4, 8
HALF, QUART, WIDE = 32, 16, 1024
PLANE = 256


def rem(a, b):
    return lax.rem(a, jnp.int32(b))


def div(a, b):
    return lax.div(a, jnp.int32(b))


def coords():
    b = lax.axis_index("blk")
    k = lax.axis_index("cls")
    z, h, c = div(b, 4), rem(div(b, 2), 2), rem(b, 2)
    x, low = div(k, 2), rem(k, 2)
    return b, k, x, 2 * h + low, z, c


def device(x, y, z, c):
    return (z * 4 + div(y, 2) * 2 + c, x * 2 + rem(y, 2))


def lse_of(parts):
    m = parts[0]
    for v in parts[1:]:
        m = jnp.maximum(m, v)
    s = jnp.exp(parts[0] - m)
    for v in parts[1:]:
        s = s + jnp.exp(v - m)
    return m + jnp.log(s)


def gather_kernel(
    off_ref, feat_hbm, lab_ref, other_ref, w_hbm,
    f_ref, d_ref, own_ref,
    w_ref, lt_ref, msg, got_p, msg_z, got_z, msg_c, got_c,
    wsem, lsem, isem, isend, zsem, zsend, xysem, xysend, dsem, dsend, csem, csend,
    psem, psend, z2sem, z2send, c2sem, c2send,
):
    b, k, x, y, z, c = coords()
    par, low, high = rem(x, 2), rem(y, 2), div(y, 2)
    up, down = rem(z + 1, Z), rem(z + Z - 1, Z)
    xr, xl = rem(x + 1, X), rem(x + X - 1, X)
    yr, yl = rem(y + 1, Y), rem(y + Y - 1, Y)
    sibling = device(x, y, z, 1 - c)

    plane_peers = [
        device(rem(x + i // 4, X), rem(y + i % 4, Y), z, c) for i in range(1, 16)
    ]
    z_peers = [device(x, y, rem(z + i, Z), c) for i in range(1, 8)]
    cross = device(x, 3 - y, z, 1 - c)

    w_copy = pltpu.make_async_copy(w_hbm, w_ref, wsem)
    w_copy.start()

    barrier = pltpu.get_barrier_semaphore()
    for peer in plane_peers + z_peers + [sibling, cross]:
        pl.semaphore_signal(barrier, inc=1, device_id=peer, device_id_type=MESH)
    pl.semaphore_wait(barrier, 24)

    def rows(start, size):
        return pl.ds(pl.multiple_of(start, 16), size)

    def unit(zz, hh, cc, half):
        return zz * PLANE + hh * 128 + cc * 64 + half * HALF

    def send(src, dst, ssem, rsem, dev):
        return pltpu.make_async_remote_copy(
            src_ref=src, dst_ref=dst, send_sem=ssem, recv_sem=rsem,
            device_id=dev, device_id_type=MESH,
        )

    first = unit(z, low, par, c)
    holder = par == c
    mine = low == high

    def first_to(i, dev):
        start = unit(z, high, c, i)
        return send(
            feat_hbm.at[pl.ds(i * HALF, HALF), :], f_ref.at[rows(start, HALF), :],
            isend.at[i], isem, dev,
        )

    def first_local(i):
        start = unit(z, high, c, i)
        return pltpu.make_async_copy(
            feat_hbm.at[pl.ds(i * HALF, HALF), :], f_ref.at[rows(start, HALF), :], lsem
        )

    for i in range(2):
        @pl.when(jnp.logical_and(holder, mine))
        def _():
            @pl.when(c == i)
            def _():
                first_local(i).start()

            @pl.when(c != i)
            def _():
                first_to(i, sibling).start()

        @pl.when(jnp.logical_and(holder, jnp.logical_not(mine)))
        def _():
            first_to(i, device(x, 3 - y, z, jnp.int32(i))).start()

    for i in range(2):
        @pl.when(jnp.logical_and(jnp.logical_and(holder, mine), c == i))
        def _():
            first_local(i).wait()

    @pl.when(jnp.logical_not(jnp.logical_and(holder, mine)))
    def _():
        at = f_ref.at[rows(first, HALF), :]
        send(at, at, isend.at[0], isem, sibling).wait_recv()

    w_copy.wait()

    def plane_of(j):
        step = div(j + 1, 2)
        return rem(jnp.where(rem(j, 2) == 1, z - step, z + step) + Z, Z)

    def piece(start, size):
        return f_ref.at[rows(start, size), :]

    def to_z(zz, start, size, slot, dev):
        at = piece(start, size)
        return send(at, at, zsend.at[slot], zsem.at[zz], dev)

    def to_xy(zz, start, i):
        dev = [
            device(xr, y, z, c), device(xl, y, z, c), device(x, yr, z, c), device(x, yl, z, c),
        ][i]
        at = piece(start + (i % 2) * QUART, QUART)
        return send(at, at, xysend.at[i, zz], xysem.at[i, zz], dev)

    def to_diag(zz, i):
        if i < 2:
            dev = device(x, yr if i == 0 else yl, z, c)
            start, cols = unit(zz, low, 1 - par, c), 0
        else:
            dev = device(xr if i == 2 else xl, y, z, c)
            start, cols = unit(zz, 1 - low, par, c), WIDE
        at = f_ref.at[rows(start + (i % 2) * QUART, QUART), pl.ds(cols, WIDE)]
        return send(at, at, dsend.at[i, zz], dsem.at[zz], dev)

    def to_sibling(zz, i):
        hh = low if i in (0, 1) else 1 - low
        cc = par if i in (0, 2) else 1 - par
        at = piece(unit(zz, hh, cc, c), HALF)
        return send(at, at, csend.at[i, zz], csem.at[zz], sibling)

    up_dev, down_dev = device(x, y, up, c), device(x, y, down, c)

    def step(n, carry):
        @pl.when(n < 8)
        def _():
            j = n
            zz = plane_of(j)
            start = unit(zz, low, par, c)

            @pl.when(j > 0)
            def _():
                to_z(zz, start, HALF, 0, up_dev).wait_recv()

            odd = rem(j, 2) == 1

            @pl.when(jnp.logical_or(j == 0, jnp.logical_and(odd, j < 5)))
            def _():
                to_z(zz, start, HALF, div(j + 1, 2), up_dev).start()

            @pl.when(jnp.logical_and(jnp.logical_not(odd), j < 5))
            def _():
                to_z(zz, start, HALF, 4 + div(j, 2), down_dev).start()

            @pl.when(j == 5)
            def _():
                to_z(zz, start, QUART, 3, up_dev).start()

            @pl.when(j == 6)
            def _():
                to_z(zz, start + QUART, QUART, 7, down_dev).start()

            for i in range(4):
                to_xy(zz, start, i).start()
            to_sibling(zz, 0).start()

        @pl.when(jnp.logical_and(n >= 1, n < 9))
        def _():
            zz = plane_of(n - 1)
            for i in range(4):
                src = unit(zz, low, 1 - par, c) if i < 2 else unit(zz, 1 - low, par, c)
                to_xy(zz, src, i).wait_recv()
            for i in range(4):
                to_diag(zz, i).start()
            to_sibling(zz, 1).start()
            to_sibling(zz, 2).start()

        @pl.when(jnp.logical_and(n >= 2, n < 10))
        def _():
            zz = plane_of(n - 2)
            at = piece(unit(zz, 1 - low, 1 - par, c), HALF)
            send(at, at, dsend.at[0, zz], dsem.at[zz], sibling).wait_recv()
            to_sibling(zz, 3).start()

        @pl.when(n >= 3)
        def _():
            zz = plane_of(n - 3)
            at = piece(zz * PLANE, 128)
            send(at, at, csend.at[0, zz], csem.at[zz], sibling).wait_recv()
            cols = pl.ds(pl.multiple_of(zz * PLANE, PLANE), PLANE)
            lt = lax.dot_general(
                w_ref[...], f_ref[cols, :], (((1,), (1,)), ((), ())),
                preferred_element_type=jnp.float32,
            )
            lt_ref[:, cols] = lt
            m = jnp.max(lt, axis=0, keepdims=True)
            s = jnp.sum(jnp.exp(lt - m), axis=0, keepdims=True)
            msg[0:1, cols] = m + jnp.log(s)

        return carry

    lax.fori_loop(0, 11, step, 0)

    lane = lax.broadcasted_iota(jnp.int32, (1, 2048), 1)
    msg[1:2, :] = jnp.where(div(lane, 64) == b, lab_ref[...].astype(jnp.float32), -1.0)

    def exchange(src, dst, ssems, rsems, peers):
        copies = [
            send(src, dst.at[i], ssems.at[i], rsems.at[i], peer) for i, peer in enumerate(peers)
        ]
        for copy in copies:
            copy.start()
        for copy in copies:
            copy.wait()

    def merged(src, dst, n):
        lse = lse_of([src[0:1, :]] + [dst[i, 0:1, :] for i in range(n)])
        lab = src[1:2, :]
        for i in range(n):
            lab = jnp.maximum(lab, dst[i, 1:2, :])
        return lse, lab

    exchange(msg, got_p, psend, psem, plane_peers)
    lse, lab = merged(msg, got_p, 15)
    msg_z[0:1, :] = lse
    msg_z[1:2, :] = lab
    exchange(msg_z, got_z, z2send, z2sem, z_peers)
    lse, lab = merged(msg_z, got_z, 7)
    msg_c[0:1, :] = lse
    msg_c[1:2, :] = lab
    exchange(msg_c, got_c, c2send, c2sem, [sibling])
    slab, lab = merged(msg_c, got_c, 1)
    other = other_ref[...]
    high_lse = jnp.maximum(slab, other)
    lse = high_lse + jnp.log(jnp.exp(slab - high_lse) + jnp.exp(other - high_lse))
    msg[0:1, :] = lse
    msg[1:2, :] = lab
    at = msg[0:1, pl.ds(pl.multiple_of(div(b, 2) * 128, 128), 128)]
    own_ref[...] = jnp.where(rem(b, 2) == 1, at[:, 64:], at[:, :64])

    base = off_ref[0] + (b * 8 + k) * 512

    def delta(n, carry):
        cols = pl.ds(pl.multiple_of(n * PLANE, PLANE), PLANE)
        local = msg[1:2, cols].astype(jnp.int32) - base
        hot = lax.broadcasted_iota(jnp.int32, (512, PLANE), 0) == local
        p = jnp.exp(lt_ref[:, cols] - msg[0:1, cols])
        d_ref[:, cols] = (p - jnp.where(hot, 1.0, 0.0)).astype(jnp.bfloat16)
        return carry

    lax.fori_loop(0, 8, delta, 0)

    for i in range(2):
        @pl.when(jnp.logical_and(holder, jnp.logical_not(jnp.logical_and(mine, c == i))))
        def _():
            first_to(i, sibling).wait_send()
    for slot in range(8):
        to_z(z, first, QUART if slot in (3, 7) else HALF, slot, up_dev).wait_send()

    def drain(zz, carry):
        for i in range(4):
            to_xy(zz, first, i).wait_send()
            to_diag(zz, i).wait_send()
            to_sibling(zz, i).wait_send()
        return carry

    lax.fori_loop(0, 8, drain, 0)


def gather(offset, features, labels, other, weight):
    dma = pltpu.SemaphoreType.DMA
    any_spec = pl.BlockSpec(memory_space=pl.ANY)
    vmem = pl.BlockSpec(memory_space=pltpu.VMEM)
    return pl.pallas_call(
        gather_kernel,
        out_shape=(
            jax.ShapeDtypeStruct((2048, 2048), jnp.bfloat16),
            jax.ShapeDtypeStruct((512, 2048), jnp.bfloat16),
            jax.ShapeDtypeStruct((1, 64), jnp.float32),
        ),
        in_specs=[pl.BlockSpec(memory_space=pltpu.SMEM), any_spec, vmem, vmem, any_spec],
        out_specs=(vmem, vmem, vmem),
        scratch_shapes=[
            pltpu.VMEM((512, 2048), jnp.bfloat16),
            pltpu.VMEM((512, 2048), jnp.float32),
            pltpu.VMEM((2, 2048), jnp.float32),
            pltpu.VMEM((15, 2, 2048), jnp.float32),
            pltpu.VMEM((2, 2048), jnp.float32),
            pltpu.VMEM((7, 2, 2048), jnp.float32),
            pltpu.VMEM((2, 2048), jnp.float32),
            pltpu.VMEM((1, 2, 2048), jnp.float32),
            dma, dma, dma, dma((2,)), dma((8,)), dma((8,)),
            dma((4, 8)), dma((4, 8)), dma((8,)), dma((4, 8)), dma((8,)), dma((4, 8)),
            dma((15,)), dma((15,)), dma((7,)), dma((7,)), dma((1,)), dma((1,)),
        ],
        compiler_params=pltpu.CompilerParams(
            collective_id=0, has_side_effects=True, vmem_limit_bytes=40 << 20
        ),
    )(offset, features, labels, other, weight)


def update_kernel(d_ref, f_ref, w_ref, a_ref, nw_ref, na_ref):
    grad = jnp.dot(d_ref[...], f_ref[...], preferred_element_type=jnp.float32)
    acc = a_ref[...] + grad * grad
    na_ref[...] = acc
    step = 0.05 * grad / (jnp.sqrt(acc) + 1e-10)
    nw_ref[...] = (w_ref[...].astype(jnp.float32) - step).astype(jnp.bfloat16)


def update(delta, rows, weight, accum, tile=256):
    col = lambda i: (0, i)
    return pl.pallas_call(
        update_kernel,
        grid=(2048 // tile,),
        out_shape=(
            jax.ShapeDtypeStruct((512, 2048), jnp.bfloat16),
            jax.ShapeDtypeStruct((512, 2048), jnp.float32),
        ),
        in_specs=[
            pl.BlockSpec((512, 2048), lambda i: (0, 0)),
            pl.BlockSpec((2048, tile), col),
            pl.BlockSpec((512, tile), col),
            pl.BlockSpec((512, tile), col),
        ],
        out_specs=(pl.BlockSpec((512, tile), col), pl.BlockSpec((512, tile), col)),
        compiler_params=pltpu.CompilerParams(vmem_limit_bytes=24 << 20),
    )(delta, rows, weight, accum)


def body(features, labels, offset, other_lse, weight, accum):
    tiled = jnp.tile(labels, 32).reshape(1, 2048)
    rows, delta, own = gather(offset, features, tiled, other_lse.reshape(1, 2048), weight)
    new_weight, new_accum = update(delta, rows, weight, accum)
    return (new_weight, new_accum, own.reshape(64))


def solution(mesh):
    in_specs = (
        P("blk", None),
        P("blk"),
        P(),
        P(),
        P(("blk", "cls"), None),
        P(("blk", "cls"), None),
    )
    out_specs = (P(("blk", "cls"), None), P(("blk", "cls"), None), P("blk"))
    return jax.shard_map(body, mesh=mesh, in_specs=in_specs, out_specs=out_specs, check_vma=False)
```

```python
import jax
import jax.numpy as jnp
from jax import lax
from jax.experimental import pallas as pl
from jax.experimental.pallas import tpu as pltpu
from jax.sharding import PartitionSpec as P

MESH = pl.DeviceIdType.MESH
X, Y, Z = 4, 4, 8
HALF, QUART, WIDE = 32, 16, 1024
PLANE = 256
OFFSET = (0, -1, 1, -2, 2, -3, 3, 4)
SLOT = {o % Z: j for j, o in enumerate(OFFSET)}
LANES = 128


def rem(a, b):
    return lax.rem(a, jnp.int32(b))


def div(a, b):
    return lax.div(a, jnp.int32(b))


def coords():
    b = lax.axis_index("blk")
    k = lax.axis_index("cls")
    z, h, c = div(b, 4), rem(div(b, 2), 2), rem(b, 2)
    x, low = div(k, 2), rem(k, 2)
    return b, k, x, 2 * h + low, z, c


def device(x, y, z, c):
    return (z * 4 + div(y, 2) * 2 + c, x * 2 + rem(y, 2))


def lse_of(parts):
    m = parts[0]
    for v in parts[1:]:
        m = jnp.maximum(m, v)
    s = jnp.exp(parts[0] - m)
    for v in parts[1:]:
        s = s + jnp.exp(v - m)
    return m + jnp.log(s)


def max_of(parts):
    m = parts[0]
    for v in parts[1:]:
        m = jnp.maximum(m, v)
    return m


def gather_kernel(
    off_ref, feat_hbm, lab_hbm, other_hbm, w_hbm, a_hbm,
    f_ref, d_ref, w_ref, a_ref, own_ref,
    lab_ref, other_ref, lt_ref, msg, got_p, msg_z, got_z, msg_c, got_c,
    wsem, asem, osem, lsem, isem, isend, zsem, zsend, xysem, xysend, dsem, dsend, csem, csend,
    psem, psend, z2sem, z2send, c2sem, c2send,
):
    b, k, x, y, z, c = coords()
    par, low, high = rem(x, 2), rem(y, 2), div(y, 2)
    up, down = rem(z + 1, Z), rem(z + Z - 1, Z)
    xr, xl = rem(x + 1, X), rem(x + X - 1, X)
    yr, yl = rem(y + 1, Y), rem(y + Y - 1, Y)
    sibling = device(x, y, z, 1 - c)
    up_dev, down_dev = device(x, y, up, c), device(x, y, down, c)
    xr_dev, xl_dev = device(xr, y, z, c), device(xl, y, z, c)
    yr_dev, yl_dev = device(x, yr, z, c), device(x, yl, z, c)
    cross = device(x, 3 - y, z, 1 - c)

    plane_peers = [
        device(rem(x + i // 4, X), rem(y + i % 4, Y), z, c) for i in range(1, 16)
    ]
    z_peers = [device(x, y, rem(z + i, Z), c) for i in range(1, 8)]

    w_copy = pltpu.make_async_copy(w_hbm, w_ref, wsem)
    w_copy.start()
    a_copy = pltpu.make_async_copy(a_hbm, a_ref, asem)
    a_copy.start()
    lab_copy = pltpu.make_async_copy(lab_hbm, lab_ref, osem.at[0])
    lab_copy.start()
    other_copy = pltpu.make_async_copy(other_hbm, other_ref, osem.at[1])
    other_copy.start()

    barrier = pltpu.get_barrier_semaphore()
    near = [xr_dev, xl_dev, yr_dev, yl_dev, up_dev, down_dev, sibling, cross]
    for peer in near:
        pl.semaphore_signal(barrier, inc=1, device_id=peer, device_id_type=MESH)
    pl.semaphore_wait(barrier, len(near))

    def rows(start, size):
        return pl.ds(pl.multiple_of(start, 16), size)

    def unit(hh, cc):
        return hh * 128 + cc * 64 + c * HALF

    mine_at = unit(low, par)
    x_at = unit(low, 1 - par)
    y_at = unit(1 - low, par)
    diag_at = unit(1 - low, 1 - par)

    def send(src, dst, ssem, rsem, dev):
        return pltpu.make_async_remote_copy(
            src_ref=src, dst_ref=dst, send_sem=ssem, recv_sem=rsem,
            device_id=dev, device_id_type=MESH,
        )

    holder = par == c
    mine = low == high

    def first_refs(i, q):
        start = high * 128 + c * 64 + i * HALF + q * QUART
        return (
            feat_hbm.at[pl.ds(i * HALF + q * QUART, QUART), :],
            f_ref.at[0, rows(start, QUART), :],
        )

    def first_to(i, q, dev):
        src, dst = first_refs(i, q)
        return send(src, dst, isend.at[i, q], isem.at[q], dev)

    def first_local(i, q):
        src, dst = first_refs(i, q)
        return pltpu.make_async_copy(src, dst, lsem.at[q])

    local = jnp.logical_and(holder, mine)
    for q in range(2):
        for i in range(2):
            @pl.when(jnp.logical_and(local, c == i))
            def _():
                first_local(i, q).start()

            @pl.when(jnp.logical_and(local, c != i))
            def _():
                first_to(i, q, sibling).start()

            @pl.when(jnp.logical_and(holder, jnp.logical_not(mine)))
            def _():
                first_to(i, q, device(x, 3 - y, z, jnp.int32(i))).start()

    def first_wait(q):
        for i in range(2):
            @pl.when(jnp.logical_and(local, c == i))
            def _():
                first_local(i, q).wait()

        @pl.when(jnp.logical_not(local))
        def _():
            at = f_ref.at[0, rows(mine_at + q * QUART, QUART), :]
            send(at, at, isend.at[0, q], isem.at[q], sibling).wait_recv()

    def piece(slot, start, size):
        return f_ref.at[slot, rows(start, size), :]

    def to_z(slot, dst_slot, q, dev):
        start = mine_at + q * QUART
        return send(
            piece(slot, start, QUART), piece(dst_slot, start, QUART),
            zsend.at[dst_slot, q], zsem.at[dst_slot, q], dev,
        )

    def z_wait(slot, q):
        to_z(slot, slot, q, up_dev).wait_recv()

    def region(s, n, start, size, cols=slice(None)):
        lo = max(2 * s - 1, 0) if isinstance(s, int) else jnp.maximum(2 * s - 1, 0)
        return f_ref.at[pl.ds(lo, n), rows(start, size), cols]

    def to_xy(s, n, i, start):
        at = region(s, n, start + (i % 2) * QUART, QUART)
        dev = (xr_dev, xl_dev, yr_dev, yl_dev)[i]
        return send(at, at, xysend.at[i, s], xysem.at[i, s], dev)

    def to_diag(s, n, i):
        start, cols = (x_at, 0) if i < 2 else (y_at, WIDE)
        at = region(s, n, start + (i % 2) * QUART, QUART, pl.ds(cols, WIDE))
        dev = (yr_dev, yl_dev, xr_dev, xl_dev)[i]
        return send(at, at, dsend.at[i, s], dsem.at[i, s], dev)

    def diag_wait(s, n, i):
        cols = 0 if i < 2 else WIDE
        at = region(s, n, diag_at + (i % 2) * QUART, QUART, pl.ds(cols, WIDE))
        send(at, at, dsend.at[i, s], dsem.at[i, s], sibling).wait_recv()

    def to_sibling(s, n, i):
        at = region(s, n, (mine_at, x_at, y_at, diag_at)[i], HALF)
        return send(at, at, csend.at[i, s], csem.at[i, s], sibling)

    def each(s, go):
        pair = jnp.logical_and(s > 0, s < 4)
        pl.when(pair)(lambda: go(s, 2))
        pl.when(jnp.logical_not(pair))(lambda: go(s, 1))

    def step(n, carry):
        @pl.when(n < 5)
        def _():
            for q in range(2):
                @pl.when(n == 0)
                def _():
                    first_wait(q)
                    to_z(0, 1, q, up_dev).start()
                    to_z(0, 2, q, down_dev).start()

                @pl.when(jnp.logical_and(n > 0, n < 3))
                def _():
                    z_wait(2 * n - 1, q)
                    to_z(2 * n - 1, 2 * n + 1, q, up_dev).start()
                    z_wait(2 * n, q)
                    to_z(2 * n, 2 * n + 2, q, down_dev).start()

                @pl.when(n == 3)
                def _():
                    z_wait(5, q)
                    z_wait(6, q)
                    if q == 0:
                        to_z(5, 7, 0, up_dev).start()
                    else:
                        to_z(6, 7, 1, down_dev).start()

                @pl.when(n == 4)
                def _():
                    z_wait(7, q)

            def go(s, m):
                for i in range(4):
                    to_xy(s, m, i, mine_at).start()
                to_sibling(s, m, 0).start()

            each(n, go)

        @pl.when(jnp.logical_and(n >= 1, n < 6))
        def _():
            def go(s, m):
                for i in range(4):
                    to_xy(s, m, i, x_at if i < 2 else y_at).wait_recv()
                    to_diag(s, m, i).start()
                to_sibling(s, m, 1).start()
                to_sibling(s, m, 2).start()

            each(n - 1, go)

        @pl.when(jnp.logical_and(n >= 2, n < 7))
        def _():
            def go(s, m):
                for i in range(4):
                    diag_wait(s, m, i)
                to_sibling(s, m, 3).start()

            each(n - 2, go)

        @pl.when(n == 3)
        def _():
            w_copy.wait()

        @pl.when(n >= 3)
        def _():
            s = n - 3

            def go(s, m):
                for i in range(4):
                    to_sibling(s, m, i).wait_recv()

            each(s, go)

            def scores(slot, carry):
                lt = lax.dot_general(
                    w_ref[...], f_ref[slot], (((1,), (1,)), ((), ())),
                    preferred_element_type=jnp.float32,
                )
                lt_ref[slot] = lt
                m = jnp.max(lt, axis=0, keepdims=True)
                v = m + jnp.log(jnp.sum(jnp.exp(lt - m), axis=0, keepdims=True))
                msg[pl.ds(2 * slot, 1), :] = v[:, :LANES]
                msg[pl.ds(2 * slot + 1, 1), :] = v[:, LANES:]
                return carry

            lo = jnp.maximum(2 * s - 1, 0)
            hi = jnp.where(s < 4, 2 * s + 1, 8)
            lax.fori_loop(lo, hi, scores, 0)

        return carry

    lab_copy.wait()
    other_copy.wait()
    lane = lax.broadcasted_iota(jnp.int32, (16, LANES), 1)
    line = lax.broadcasted_iota(jnp.int32, (16, LANES), 0)
    twice = jnp.concatenate([lab_ref[...], lab_ref[...]], axis=1)
    own_spot = jnp.logical_and(line == high, div(lane, 64) == c)
    msg[16:32, :] = jnp.where(own_spot, twice.astype(jnp.float32), -1.0)

    lax.fori_loop(0, 8, step, 0)

    def exchange(src, dst, ssems, rsems, peers):
        copies = [
            send(src, dst.at[i], ssems.at[i], rsems.at[i], peer) for i, peer in enumerate(peers)
        ]
        for copy in copies:
            copy.start()
        for copy in copies:
            copy.wait()

    exchange(msg, got_p, psend, psem, plane_peers)
    msg_z[0:16, :] = lse_of([msg[0:16, :]] + [got_p[i, 0:16, :] for i in range(15)])
    msg_z[16:32, :] = max_of([msg[16:32, :]] + [got_p[i, 16:32, :] for i in range(15)])
    exchange(msg_z, got_z, z2send, z2sem, z_peers)
    for j, o in enumerate(OFFSET):
        for base, merge in ((0, lse_of), (16, max_of)):
            parts = [msg_z[base + 2 * j : base + 2 * j + 2, :]]
            for i in range(7):
                at = base + 2 * SLOT[(o + i + 1) % Z]
                parts.append(got_z[i, at : at + 2, :])
            msg_c[base + 2 * j : base + 2 * j + 2, :] = merge(parts)
    exchange(msg_c, got_c, c2send, c2sem, [sibling])
    slab = lse_of([msg_c[0:16, :], got_c[0, 0:16, :]])
    msg[16:32, :] = jnp.maximum(msg_c[16:32, :], got_c[0, 16:32, :])
    other = jnp.concatenate(
        [other_ref[pl.ds(2 * rem(z + o + Z, Z), 2), :] for o in OFFSET], axis=0
    )
    top = jnp.maximum(slab, other)
    msg[0:16, :] = top + jnp.log(jnp.exp(slab - top) + jnp.exp(other - top))
    at = msg[pl.ds(high, 1), :]
    own_ref[...] = jnp.where(c == 1, at[:, 64:], at[:, :64])

    base = off_ref[0] + (b * 8 + k) * 512

    def delta(slot, carry):
        def line_of(at):
            return jnp.concatenate([msg[pl.ds(at, 1), :], msg[pl.ds(at + 1, 1), :]], axis=1)

        lse, lab = line_of(2 * slot), line_of(16 + 2 * slot)
        hot = lax.broadcasted_iota(jnp.int32, (512, PLANE), 0) == lab.astype(jnp.int32) - base
        p = jnp.exp(lt_ref[slot] - lse) - jnp.where(hot, 1.0, 0.0)
        d_ref[:, pl.ds(pl.multiple_of(slot * PLANE, PLANE), PLANE)] = p.astype(jnp.bfloat16)
        return carry

    lax.fori_loop(0, 8, delta, 0)
    a_copy.wait()

    for q in range(2):
        for i in range(2):
            @pl.when(jnp.logical_and(holder, jnp.logical_not(jnp.logical_and(mine, c == i))))
            def _():
                first_to(i, q, sibling).wait_send()
        for slot in range(1, 7):
            to_z(slot, slot, q, up_dev).wait_send()
        to_z(7, 7, q, up_dev).wait_send()
    for s in range(5):
        m = 2 if 0 < s < 4 else 1
        for i in range(4):
            to_xy(s, m, i, mine_at).wait_send()
            to_diag(s, m, i).wait_send()
            to_sibling(s, m, i).wait_send()


def gather(offset, features, labels, other, weight, accum):
    dma = pltpu.SemaphoreType.DMA
    hbm = pl.BlockSpec(memory_space=pltpu.HBM)
    vmem = pl.BlockSpec(memory_space=pltpu.VMEM)
    f32 = jnp.float32
    return pl.pallas_call(
        gather_kernel,
        out_shape=(
            jax.ShapeDtypeStruct((8, PLANE, 2048), jnp.bfloat16),
            jax.ShapeDtypeStruct((512, 2048), jnp.bfloat16),
            jax.ShapeDtypeStruct((512, 2048), jnp.bfloat16),
            jax.ShapeDtypeStruct((512, 2048), f32),
            jax.ShapeDtypeStruct((1, 64), f32),
        ),
        in_specs=[pl.BlockSpec(memory_space=pltpu.SMEM)] + [hbm] * 5,
        out_specs=(vmem,) * 5,
        scratch_shapes=[
            pltpu.VMEM((1, 64), jnp.int32),
            pltpu.VMEM((16, LANES), f32),
            pltpu.VMEM((8, 512, PLANE), f32),
            pltpu.VMEM((32, LANES), f32),
            pltpu.VMEM((15, 32, LANES), f32),
            pltpu.VMEM((32, LANES), f32),
            pltpu.VMEM((7, 32, LANES), f32),
            pltpu.VMEM((32, LANES), f32),
            pltpu.VMEM((1, 32, LANES), f32),
            dma, dma, dma((2,)), dma((2,)), dma((2,)), dma((2, 2)), dma((8, 2)), dma((8, 2)),
            dma((4, 5)), dma((4, 5)), dma((4, 5)), dma((4, 5)), dma((4, 5)), dma((4, 5)),
            dma((15,)), dma((15,)), dma((7,)), dma((7,)), dma((1,)), dma((1,)),
        ],
        compiler_params=pltpu.CompilerParams(
            collective_id=0, has_side_effects=True, vmem_limit_bytes=16 << 20
        ),
    )(offset, *(pltpu.with_memory_space_constraint(v, pltpu.HBM) for v in (features, labels, other, weight, accum)))


TILE = 256
TILES = 2048 // TILE


def update_kernel(
    d_ref, f_ref, w_ref, a_ref, own_ref, nw_hbm, na_hbm, own_hbm, g_ref, nw_ref, na_ref, sem, osem
):
    own_copy = pltpu.make_async_copy(own_ref, own_hbm, osem)
    own_copy.start()

    def cols(t):
        return pl.ds(pl.multiple_of(t * TILE, TILE), TILE)

    def dot(t):
        g_ref[rem(t, 2)] = jnp.dot(
            d_ref[...], f_ref[:, cols(t)], preferred_element_type=jnp.float32
        )

    def copies(t):
        return (
            pltpu.make_async_copy(nw_ref.at[:, cols(t)], nw_hbm.at[:, cols(t)], sem.at[0, t]),
            pltpu.make_async_copy(na_ref.at[:, cols(t)], na_hbm.at[:, cols(t)], sem.at[1, t]),
        )

    def apply(t):
        grad = g_ref[rem(t, 2)]
        acc = a_ref[:, cols(t)] + grad * grad
        na_ref[:, cols(t)] = acc
        step = 0.05 * grad / (jnp.sqrt(acc) + 1e-10)
        nw_ref[:, cols(t)] = (w_ref[:, cols(t)].astype(jnp.float32) - step).astype(jnp.bfloat16)

    dot(jnp.int32(0))

    def both(t, carry):
        dot(t)
        apply(t - 1)
        for copy in copies(t - 1):
            copy.start()
        return carry

    lax.fori_loop(1, TILES, both, 0)
    apply(jnp.int32(TILES - 1))
    for copy in copies(TILES - 1):
        copy.start()
    for t in range(TILES):
        for copy in copies(t):
            copy.wait()
    own_copy.wait()


def update(delta, rows, weight, accum, own):
    vmem = pl.BlockSpec(memory_space=pltpu.VMEM)
    hbm = pl.BlockSpec(memory_space=pltpu.HBM)
    return pl.pallas_call(
        update_kernel,
        out_shape=(
            jax.ShapeDtypeStruct((512, 2048), jnp.bfloat16),
            jax.ShapeDtypeStruct((512, 2048), jnp.float32),
            jax.ShapeDtypeStruct((1, 64), jnp.float32),
        ),
        in_specs=[vmem] * 5,
        out_specs=(hbm,) * 3,
        scratch_shapes=[
            pltpu.VMEM((2, 512, TILE), jnp.float32),
            pltpu.VMEM((512, 2048), jnp.bfloat16),
            pltpu.VMEM((512, 2048), jnp.float32),
            pltpu.SemaphoreType.DMA((2, TILES)),
            pltpu.SemaphoreType.DMA,
        ],
        compiler_params=pltpu.CompilerParams(vmem_limit_bytes=16 << 20),
    )(delta, rows, weight, accum, own)


def body(features, labels, offset, other_lse, weight, accum):
    rows, delta, w, a, own = gather(
        offset, features, labels.reshape(1, 64), other_lse.reshape(16, LANES), weight, accum
    )
    new_weight, new_accum, own = update(delta, rows.reshape(2048, 2048), w, a, own)
    return (new_weight, new_accum, own.reshape(64))


def solution(mesh):
    in_specs = (
        P("blk", None),
        P("blk"),
        P(),
        P(),
        P(("blk", "cls"), None),
        P(("blk", "cls"), None),
    )
    out_specs = (P(("blk", "cls"), None), P(("blk", "cls"), None), P("blk"))
    return jax.shard_map(body, mesh=mesh, in_specs=in_specs, out_specs=out_specs, check_vma=False)
```

```python
import jax
import jax.numpy as jnp
from jax import lax
from jax.experimental import pallas as pl
from jax.experimental.pallas import tpu as pltpu
from jax.sharding import PartitionSpec as P

MESH = pl.DeviceIdType.MESH
X, Y, Z = 4, 4, 8
HALF, QUART, WIDE = 32, 16, 1024
PLANE = 256
OFFSET = (0, -1, 1, -2, 2, -3, 3, 4)
SLOT = {o % Z: j for j, o in enumerate(OFFSET)}
LANES = 128
PIECES = 4
PIECE = HALF // PIECES


def rem(a, b):
    return lax.rem(a, jnp.int32(b))


def div(a, b):
    return lax.div(a, jnp.int32(b))


def coords():
    b = lax.axis_index("blk")
    k = lax.axis_index("cls")
    z, h, c = div(b, 4), rem(div(b, 2), 2), rem(b, 2)
    x, low = div(k, 2), rem(k, 2)
    return b, k, x, 2 * h + low, z, c


def device(x, y, z, c):
    return (z * 4 + div(y, 2) * 2 + c, x * 2 + rem(y, 2))


def lse_of(parts):
    m = parts[0]
    for v in parts[1:]:
        m = jnp.maximum(m, v)
    s = jnp.exp(parts[0] - m)
    for v in parts[1:]:
        s = s + jnp.exp(v - m)
    return m + jnp.log(s)


def max_of(parts):
    m = parts[0]
    for v in parts[1:]:
        m = jnp.maximum(m, v)
    return m


def gather_kernel(
    off_ref, feat_hbm, lab_hbm, other_hbm, w_hbm, a_hbm,
    f_ref, d_ref, w_ref, a_ref, own_ref,
    lab_ref, other_ref, lt_ref, msg, got_p, msg_z, got_z, msg_c, got_c, lab, lab_p, lab_c, own_f,
    wsem, asem, osem, lsem, isem, isend, zsem, zsend, xysem, xysend, dsem, dsend, csem, csend,
    psem, psend, z2sem, z2send, c2sem, c2send, lpsem, lpsend, lzsem, lzsend, lcsem, lcsend,
):
    b, k, x, y, z, c = coords()
    par, low, high = rem(x, 2), rem(y, 2), div(y, 2)
    up, down = rem(z + 1, Z), rem(z + Z - 1, Z)
    xr, xl = rem(x + 1, X), rem(x + X - 1, X)
    yr, yl = rem(y + 1, Y), rem(y + Y - 1, Y)
    sibling = device(x, y, z, 1 - c)
    up_dev, down_dev = device(x, y, up, c), device(x, y, down, c)
    xr_dev, xl_dev = device(xr, y, z, c), device(xl, y, z, c)
    yr_dev, yl_dev = device(x, yr, z, c), device(x, yl, z, c)
    cross = device(x, 3 - y, z, 1 - c)
    diag_devs = [device(i, j, z, c) for j in (yr, yl) for i in (xr, xl)]

    plane_peers = [
        device(rem(x + i // 4, X), rem(y + i % 4, Y), z, c) for i in range(1, 16)
    ]
    z_peers = [device(x, y, rem(z + i, Z), c) for i in range(1, 8)]

    f_copy = pltpu.make_async_copy(feat_hbm, own_f, osem.at[2])
    f_copy.start()
    w_copy = pltpu.make_async_copy(w_hbm, w_ref, wsem)
    w_copy.start()
    a_copy = pltpu.make_async_copy(a_hbm, a_ref, asem)
    a_copy.start()
    lab_copy = pltpu.make_async_copy(lab_hbm, lab_ref, osem.at[0])
    lab_copy.start()
    other_copy = pltpu.make_async_copy(other_hbm, other_ref, osem.at[1])
    other_copy.start()

    barrier = pltpu.get_barrier_semaphore()
    near = [xr_dev, xl_dev, yr_dev, yl_dev, up_dev, down_dev, sibling, cross]
    for peer in near:
        pl.semaphore_signal(barrier, inc=1, device_id=peer, device_id_type=MESH)
    pl.semaphore_wait(barrier, len(near))
    f_copy.wait()

    def rows(start, size):
        return pl.ds(pl.multiple_of(start, 8), size)

    def unit(hh, cc):
        return hh * 128 + cc * 64 + c * HALF

    mine_at = unit(low, par)
    x_at = unit(low, 1 - par)
    y_at = unit(1 - low, par)
    diag_at = unit(1 - low, 1 - par)

    def send(src, dst, ssem, rsem, dev):
        return pltpu.make_async_remote_copy(
            src_ref=src, dst_ref=dst, send_sem=ssem, recv_sem=rsem,
            device_id=dev, device_id_type=MESH,
        )

    holder = par == c
    mine = low == high

    def first_refs(i, q):
        start = high * 128 + c * 64 + i * HALF + q * PIECE
        return (
            own_f.at[pl.ds(i * HALF + q * PIECE, PIECE), :],
            f_ref.at[0, rows(start, PIECE), :],
        )

    def first_to(i, q, dev):
        src, dst = first_refs(i, q)
        return send(src, dst, isend.at[i, q], isem.at[q], dev)

    def first_local(i, q):
        src, dst = first_refs(i, q)
        return pltpu.make_async_copy(src, dst, lsem.at[q])

    local = jnp.logical_and(holder, mine)
    for q in range(PIECES):
        for i in range(2):
            @pl.when(jnp.logical_and(local, c == i))
            def _():
                first_local(i, q).start()

            @pl.when(jnp.logical_and(local, c != i))
            def _():
                first_to(i, q, sibling).start()

            @pl.when(jnp.logical_and(holder, jnp.logical_not(mine)))
            def _():
                first_to(i, q, device(x, 3 - y, z, jnp.int32(i))).start()

    def first_wait(q):
        for i in range(2):
            @pl.when(jnp.logical_and(local, c == i))
            def _():
                first_local(i, q).wait()

        @pl.when(jnp.logical_not(local))
        def _():
            at = f_ref.at[0, rows(mine_at + q * PIECE, PIECE), :]
            send(at, at, isend.at[0, q], isem.at[q], sibling).wait_recv()

    def piece(slot, start, size):
        return f_ref.at[slot, rows(start, size), :]

    def to_z(slot, dst_slot, q, dev):
        start = mine_at + q * PIECE
        return send(
            piece(slot, start, PIECE), piece(dst_slot, start, PIECE),
            zsend.at[dst_slot, q], zsem.at[dst_slot, q], dev,
        )

    def z_wait(slot, q):
        to_z(slot, slot, q, up_dev).wait_recv()

    def region(s, n, start, size, cols=slice(None)):
        lo = max(2 * s - 1, 0) if isinstance(s, int) else jnp.maximum(2 * s - 1, 0)
        return f_ref.at[pl.ds(lo, n), rows(start, size), cols]

    def to_xy(s, n, i, start):
        at = region(s, n, start + (i % 2) * QUART, QUART)
        dev = (xr_dev, xl_dev, yr_dev, yl_dev)[i]
        return send(at, at, xysend.at[i, s], xysem.at[i, s], dev)

    def to_diag(s, n, i, start):
        cols = pl.ds(i // 2 * WIDE, WIDE)
        at = region(s, n, start + (i % 2) * QUART, QUART, cols)
        return send(at, at, dsend.at[i, s], dsem.at[i, s], diag_devs[i])

    def pass_on(s, n, i):
        start, cols = (x_at, 0) if i < 2 else (y_at, WIDE)
        at = region(s, n, start + (i % 2) * QUART, QUART, pl.ds(cols, WIDE))
        dev = (yr_dev, yl_dev, xr_dev, xl_dev)[i]
        return send(at, at, dsend.at[i, s], dsem.at[i, s], dev)

    def to_sibling(s, n, i):
        at = region(s, n, (mine_at, x_at, y_at, diag_at)[i], HALF)
        return send(at, at, csend.at[i, s], csem.at[i, s], sibling)

    def each(s, go):
        pair = jnp.logical_and(s > 0, s < 4)
        pl.when(pair)(lambda: go(s, 2))
        pl.when(jnp.logical_not(pair))(lambda: go(s, 1))

    lab_plane = [
        send(lab.at[0], lab_p.at[i], lpsend.at[i], lpsem.at[i], peer)
        for i, peer in enumerate(plane_peers)
    ]
    lab_z = [
        (
            send(lab.at[0], lab.at[SLOT[(-i - 1) % Z]], lzsend.at[i], lzsem.at[i], peer),
            send(lab.at[0], lab.at[SLOT[(-i - 1) % Z]], lzsend.at[i], lzsem.at[i], peer),
        )
        for i, peer in enumerate(z_peers)
    ]
    lab_sibling = send(lab, lab_c, lcsend, lcsem, sibling)

    def step(n, carry):
        @pl.when(n < 5)
        def _():
            for q in range(PIECES):
                @pl.when(n == 0)
                def _():
                    first_wait(q)
                    to_z(0, 1, q, up_dev).start()
                    to_z(0, 2, q, down_dev).start()

                @pl.when(jnp.logical_and(n > 0, n < 3))
                def _():
                    z_wait(2 * n - 1, q)
                    to_z(2 * n - 1, 2 * n + 1, q, up_dev).start()
                    z_wait(2 * n, q)
                    to_z(2 * n, 2 * n + 2, q, down_dev).start()

                @pl.when(n == 3)
                def _():
                    z_wait(5, q)
                    z_wait(6, q)
                    if q < PIECES // 2:
                        to_z(5, 7, q, up_dev).start()
                    else:
                        to_z(6, 7, q, down_dev).start()

                @pl.when(n == 4)
                def _():
                    z_wait(7, q)

            def go(s, m):
                for i in range(4):
                    to_xy(s, m, i, mine_at).start()
                to_sibling(s, m, 0).start()

            each(n, go)

        @pl.when(jnp.logical_and(n >= 1, n < 6))
        def _():
            def go(s, m):
                for i in range(4):
                    to_xy(s, m, i, x_at if i < 2 else y_at).wait_recv()
                    pass_on(s, m, i).start()
                to_sibling(s, m, 1).start()
                to_sibling(s, m, 2).start()

            each(n - 1, go)

        @pl.when(jnp.logical_and(n >= 2, n < 7))
        def _():
            def go(s, m):
                for i in range(4):
                    to_diag(s, m, i, diag_at).wait_recv()
                to_sibling(s, m, 3).start()

            each(n - 2, go)

        @pl.when(n == 5)
        def _():
            for copy in lab_plane:
                copy.start()

        @pl.when(n == 2)
        def _():
            w_copy.wait()

        @pl.when(n >= 3)
        def _():
            s = n - 3

            def go(s, m):
                for i in range(4):
                    to_sibling(s, m, i).wait_recv()

            each(s, go)

            def scores(slot, carry):
                lt = lax.dot_general(
                    w_ref[...], f_ref[slot], (((1,), (1,)), ((), ())),
                    preferred_element_type=jnp.float32,
                )
                lt_ref[slot] = lt
                m = jnp.max(lt, axis=0, keepdims=True)
                v = m + jnp.log(jnp.sum(jnp.exp(lt - m), axis=0, keepdims=True))
                msg[pl.ds(2 * slot, 1), :] = v[:, :LANES]
                msg[pl.ds(2 * slot + 1, 1), :] = v[:, LANES:]
                return carry

            lo = jnp.maximum(2 * s - 1, 0)
            hi = jnp.where(s < 4, 2 * s + 1, 8)
            lax.fori_loop(lo, hi, scores, 0)

        return carry

    lab_copy.wait()
    other_copy.wait()
    lane = lax.broadcasted_iota(jnp.int32, (2, LANES), 1)
    line = lax.broadcasted_iota(jnp.int32, (2, LANES), 0)
    twice = jnp.concatenate([lab_ref[...], lab_ref[...]], axis=1)
    own_spot = jnp.logical_and(line == high, div(lane, 64) == c)
    lab[0] = jnp.where(own_spot, twice.astype(jnp.float32), -1.0)

    lax.fori_loop(0, 8, step, 0)

    def exchange(src, dst, ssems, rsems, peers):
        copies = [
            send(src, dst.at[i], ssems.at[i], rsems.at[i], peer) for i, peer in enumerate(peers)
        ]
        for copy in copies:
            copy.start()
        for copy in copies:
            copy.wait()

    for copy in lab_plane:
        copy.wait()
    lab[0] = max_of([lab[0]] + [lab_p[i] for i in range(15)])
    for copy, _ in lab_z:
        copy.start()
    exchange(msg, got_p, psend, psem, plane_peers)
    msg_z[...] = lse_of([msg[...]] + [got_p[i] for i in range(15)])
    exchange(msg_z, got_z, z2send, z2sem, z_peers)
    for j, o in enumerate(OFFSET):
        parts = [msg_z[2 * j : 2 * j + 2, :]]
        for i in range(7):
            at = 2 * SLOT[(o + i + 1) % Z]
            parts.append(got_z[i, at : at + 2, :])
        msg_c[2 * j : 2 * j + 2, :] = lse_of(parts)
    for copy, arrived in lab_z:
        copy.wait_send()
        arrived.wait_recv()
    lab_sibling.start()
    exchange(msg_c, got_c, c2send, c2sem, [sibling])
    slab = lse_of([msg_c[...], got_c[0]])
    lab_sibling.wait()
    other = jnp.concatenate(
        [other_ref[pl.ds(2 * rem(z + o + Z, Z), 2), :] for o in OFFSET], axis=0
    )
    top = jnp.maximum(slab, other)
    msg[...] = top + jnp.log(jnp.exp(slab - top) + jnp.exp(other - top))
    at = msg[pl.ds(high, 1), :]
    own_ref[...] = jnp.where(c == 1, at[:, 64:], at[:, :64])

    base = off_ref[0] + (b * 8 + k) * 512

    def delta(slot, carry):
        lse = jnp.concatenate([msg[pl.ds(2 * slot, 1), :], msg[pl.ds(2 * slot + 1, 1), :]], axis=1)
        ids = jnp.maximum(lab[slot], lab_c[slot])
        labels = jnp.concatenate([ids[0:1, :], ids[1:2, :]], axis=1).astype(jnp.int32)
        hot = lax.broadcasted_iota(jnp.int32, (512, PLANE), 0) == labels - base
        p = jnp.exp(lt_ref[slot] - lse) - jnp.where(hot, 1.0, 0.0)
        d_ref[:, pl.ds(pl.multiple_of(slot * PLANE, PLANE), PLANE)] = p.astype(jnp.bfloat16)
        return carry

    lax.fori_loop(0, 8, delta, 0)
    a_copy.wait()

    for q in range(PIECES):
        for i in range(2):
            @pl.when(jnp.logical_and(holder, jnp.logical_not(jnp.logical_and(mine, c == i))))
            def _():
                first_to(i, q, sibling).wait_send()
        for slot in range(1, 8):
            to_z(slot, slot, q, up_dev).wait_send()
    for s in range(5):
        m = 2 if 0 < s < 4 else 1
        for i in range(4):
            to_xy(s, m, i, mine_at).wait_send()
            to_diag(s, m, i, mine_at).wait_send()
            to_sibling(s, m, i).wait_send()


def gather(offset, features, labels, other, weight, accum):
    dma = pltpu.SemaphoreType.DMA
    hbm = pl.BlockSpec(memory_space=pltpu.HBM)
    vmem = pl.BlockSpec(memory_space=pltpu.VMEM)
    f32 = jnp.float32
    return pl.pallas_call(
        gather_kernel,
        out_shape=(
            jax.ShapeDtypeStruct((8, PLANE, 2048), jnp.bfloat16),
            jax.ShapeDtypeStruct((512, 2048), jnp.bfloat16),
            jax.ShapeDtypeStruct((512, 2048), jnp.bfloat16),
            jax.ShapeDtypeStruct((512, 2048), f32),
            jax.ShapeDtypeStruct((1, 64), f32),
        ),
        in_specs=[pl.BlockSpec(memory_space=pltpu.SMEM)] + [hbm] * 5,
        out_specs=(vmem,) * 5,
        scratch_shapes=[
            pltpu.VMEM((1, 64), jnp.int32),
            pltpu.VMEM((16, LANES), f32),
            pltpu.VMEM((8, 512, PLANE), f32),
            pltpu.VMEM((16, LANES), f32),
            pltpu.VMEM((15, 16, LANES), f32),
            pltpu.VMEM((16, LANES), f32),
            pltpu.VMEM((7, 16, LANES), f32),
            pltpu.VMEM((16, LANES), f32),
            pltpu.VMEM((1, 16, LANES), f32),
            pltpu.VMEM((8, 2, LANES), f32),
            pltpu.VMEM((15, 2, LANES), f32),
            pltpu.VMEM((8, 2, LANES), f32),
            pltpu.VMEM((64, 2048), jnp.bfloat16),
            dma, dma, dma((3,)), dma((PIECES,)), dma((PIECES,)), dma((2, PIECES)),
            dma((8, PIECES)), dma((8, PIECES)),
            dma((4, 5)), dma((4, 5)), dma((4, 5)), dma((4, 5)), dma((4, 5)), dma((4, 5)),
            dma((15,)), dma((15,)), dma((7,)), dma((7,)), dma((1,)), dma((1,)),
            dma((15,)), dma((15,)), dma((7,)), dma((7,)), dma, dma,
        ],
        compiler_params=pltpu.CompilerParams(
            collective_id=0, has_side_effects=True, vmem_limit_bytes=16 << 20
        ),
    )(offset, *(pltpu.with_memory_space_constraint(v, pltpu.HBM) for v in (features, labels, other, weight, accum)))


TILES = ((0, 1024), (1024, 512), (1536, 512))


def update_kernel(
    d_ref, f_ref, w_ref, a_ref, own_ref, nw_hbm, na_hbm, own_hbm, nw_ref, na_ref, sem, osem
):
    own_copy = pltpu.make_async_copy(own_ref, own_hbm, osem)
    own_copy.start()

    def copies(t):
        cols = pl.ds(*TILES[t])
        return (
            pltpu.make_async_copy(nw_ref.at[:, cols], nw_hbm.at[:, cols], sem.at[0, t]),
            pltpu.make_async_copy(na_ref.at[:, cols], na_hbm.at[:, cols], sem.at[1, t]),
        )

    for t, (at, size) in enumerate(TILES):
        cols = pl.ds(at, size)
        grad = jnp.dot(d_ref[...], f_ref[:, cols], preferred_element_type=jnp.float32)
        acc = a_ref[:, cols] + grad * grad
        na_ref[:, cols] = acc
        step = 0.05 * grad / (acc * lax.rsqrt(acc) + 1e-10)
        nw_ref[:, cols] = (w_ref[:, cols].astype(jnp.float32) - step).astype(jnp.bfloat16)
        for copy in copies(t):
            copy.start()
    for t in range(len(TILES)):
        for copy in copies(t):
            copy.wait()
    own_copy.wait()


def update(delta, rows, weight, accum, own):
    vmem = pl.BlockSpec(memory_space=pltpu.VMEM)
    hbm = pl.BlockSpec(memory_space=pltpu.HBM)
    return pl.pallas_call(
        update_kernel,
        out_shape=(
            jax.ShapeDtypeStruct((512, 2048), jnp.bfloat16),
            jax.ShapeDtypeStruct((512, 2048), jnp.float32),
            jax.ShapeDtypeStruct((1, 64), jnp.float32),
        ),
        in_specs=[vmem] * 5,
        out_specs=(hbm,) * 3,
        scratch_shapes=[
            pltpu.VMEM((512, 2048), jnp.bfloat16),
            pltpu.VMEM((512, 2048), jnp.float32),
            pltpu.SemaphoreType.DMA((2, len(TILES))),
            pltpu.SemaphoreType.DMA,
        ],
        compiler_params=pltpu.CompilerParams(vmem_limit_bytes=16 << 20),
    )(delta, rows, weight, accum, own)


def body(features, labels, offset, other_lse, weight, accum):
    rows, delta, w, a, own = gather(
        offset, features, labels.reshape(1, 64), other_lse.reshape(16, LANES), weight, accum
    )
    new_weight, new_accum, own = update(delta, rows.reshape(2048, 2048), w, a, own)
    return (new_weight, new_accum, own.reshape(64))


def solution(mesh):
    in_specs = (
        P("blk", None),
        P("blk"),
        P(),
        P(),
        P(("blk", "cls"), None),
        P(("blk", "cls"), None),
    )
    out_specs = (P(("blk", "cls"), None), P(("blk", "cls"), None), P("blk"))
    return jax.shard_map(body, mesh=mesh, in_specs=in_specs, out_specs=out_specs, check_vma=False)
```

```python
import jax
import jax.numpy as jnp
from jax import lax
from jax.experimental import pallas as pl
from jax.experimental.pallas import tpu as pltpu
from jax.sharding import PartitionSpec as P

MESH = pl.DeviceIdType.MESH
X, Y, Z = 4, 4, 8
HALF, QUART, WIDE = 32, 16, 1024
PLANE = 256
OFFSET = (0, -1, 1, -2, 2, -3, 3, 4)
SLOT = {o % Z: j for j, o in enumerate(OFFSET)}
LANES = 128
PIECES = 4
PIECE = HALF // PIECES


def rem(a, b):
    return lax.rem(a, jnp.int32(b))


def div(a, b):
    return lax.div(a, jnp.int32(b))


def coords():
    b = lax.axis_index("blk")
    k = lax.axis_index("cls")
    z, h, c = div(b, 4), rem(div(b, 2), 2), rem(b, 2)
    x, low = div(k, 2), rem(k, 2)
    return b, k, x, 2 * h + low, z, c


def device(x, y, z, c):
    return (z * 4 + div(y, 2) * 2 + c, x * 2 + rem(y, 2))


def lse_of(parts):
    m = parts[0]
    for v in parts[1:]:
        m = jnp.maximum(m, v)
    s = jnp.exp(parts[0] - m)
    for v in parts[1:]:
        s = s + jnp.exp(v - m)
    return m + jnp.log(s)


def max_of(parts):
    m = parts[0]
    for v in parts[1:]:
        m = jnp.maximum(m, v)
    return m


def gather_kernel(
    off_ref, feat_hbm, lab_hbm, other_hbm, w_hbm, a_hbm,
    f_ref, d_ref, w_ref, a_ref, own_ref,
    lab_ref, other_ref, lt_ref, msg, got_p, msg_z, got_z, fin, lab, lab_p, lab_c, own_f, w_sib, lt_out,
    wsem, asem, osem, lsem, isem, isend, zsem, zsend, xysem, xysend, dsem, dsend, csem, csend,
    psem, psend, z2sem, z2send, c2sem, c2send, lpsem, lpsend, lzsem, lzsend, lcsem, lcsend,
    wxsem, wxsend, ltsem, ltsend,
):
    b, k, x, y, z, c = coords()
    par, low, high = rem(x, 2), rem(y, 2), div(y, 2)
    up, down = rem(z + 1, Z), rem(z + Z - 1, Z)
    xr, xl = rem(x + 1, X), rem(x + X - 1, X)
    yr, yl = rem(y + 1, Y), rem(y + Y - 1, Y)
    sibling = device(x, y, z, 1 - c)
    up_dev, down_dev = device(x, y, up, c), device(x, y, down, c)
    xr_dev, xl_dev = device(xr, y, z, c), device(xl, y, z, c)
    yr_dev, yl_dev = device(x, yr, z, c), device(x, yl, z, c)
    cross = device(x, 3 - y, z, 1 - c)
    diag_devs = [device(i, j, z, c) for j in (yr, yl) for i in (xr, xl)]

    plane_peers = [
        device(rem(x + i // 4, X), rem(y + i % 4, Y), z, c) for i in range(1, 16)
    ]
    z_peers = [device(x, y, rem(z + i, Z), c) for i in range(1, 8)]

    f_copy = pltpu.make_async_copy(feat_hbm, own_f, osem.at[2])
    f_copy.start()
    w_copy = pltpu.make_async_copy(w_hbm, w_ref, wsem)
    w_copy.start()
    a_copy = pltpu.make_async_copy(a_hbm, a_ref, asem)
    a_copy.start()
    lab_copy = pltpu.make_async_copy(lab_hbm, lab_ref, osem.at[0])
    lab_copy.start()
    other_copy = pltpu.make_async_copy(other_hbm, other_ref, osem.at[1])
    other_copy.start()

    barrier = pltpu.get_barrier_semaphore()
    near = [xr_dev, xl_dev, yr_dev, yl_dev, up_dev, down_dev, sibling, cross]
    for peer in near:
        pl.semaphore_signal(barrier, inc=1, device_id=peer, device_id_type=MESH)
    pl.semaphore_wait(barrier, len(near))
    f_copy.wait()

    def rows(start, size):
        return pl.ds(pl.multiple_of(start, 8), size)

    def unit(hh, cc):
        return c * 128 + (hh * 2 + cc) * HALF

    mine_at = unit(low, par)
    x_at = unit(low, 1 - par)
    y_at = unit(1 - low, par)
    diag_at = unit(1 - low, 1 - par)

    def send(src, dst, ssem, rsem, dev):
        return pltpu.make_async_remote_copy(
            src_ref=src, dst_ref=dst, send_sem=ssem, recv_sem=rsem,
            device_id=dev, device_id_type=MESH,
        )

    holder = par == c
    mine = low == high

    def first_refs(i, q):
        start = i * 128 + (high * 2 + c) * HALF + q * PIECE
        return (
            own_f.at[pl.ds(i * HALF + q * PIECE, PIECE), :],
            f_ref.at[0, rows(start, PIECE), :],
        )

    def first_to(i, q, dev):
        src, dst = first_refs(i, q)
        return send(src, dst, isend.at[i, q], isem.at[q], dev)

    def first_local(i, q):
        src, dst = first_refs(i, q)
        return pltpu.make_async_copy(src, dst, lsem.at[q])

    local = jnp.logical_and(holder, mine)
    for q in range(PIECES):
        for i in range(2):
            @pl.when(jnp.logical_and(local, c == i))
            def _():
                first_local(i, q).start()

            @pl.when(jnp.logical_and(local, c != i))
            def _():
                first_to(i, q, sibling).start()

            @pl.when(jnp.logical_and(holder, jnp.logical_not(mine)))
            def _():
                first_to(i, q, device(x, 3 - y, z, jnp.int32(i))).start()

    def first_wait(q):
        for i in range(2):
            @pl.when(jnp.logical_and(local, c == i))
            def _():
                first_local(i, q).wait()

        @pl.when(jnp.logical_not(local))
        def _():
            at = f_ref.at[0, rows(mine_at + q * PIECE, PIECE), :]
            send(at, at, isend.at[0, q], isem.at[q], sibling).wait_recv()

    def piece(slot, start, size):
        return f_ref.at[slot, rows(start, size), :]

    def to_z(slot, dst_slot, q, dev):
        start = mine_at + q * PIECE
        return send(
            piece(slot, start, PIECE), piece(dst_slot, start, PIECE),
            zsend.at[dst_slot, q], zsem.at[dst_slot, q], dev,
        )

    def z_wait(slot, q):
        to_z(slot, slot, q, up_dev).wait_recv()

    def region(s, n, start, size, cols=slice(None)):
        lo = max(2 * s - 1, 0) if isinstance(s, int) else jnp.maximum(2 * s - 1, 0)
        return f_ref.at[pl.ds(lo, n), rows(start, size), cols]

    def to_xy(s, n, i, start):
        at = region(s, n, start + (i % 2) * QUART, QUART)
        dev = (xr_dev, xl_dev, yr_dev, yl_dev)[i]
        return send(at, at, xysend.at[i, s], xysem.at[i, s], dev)

    def to_diag(s, n, i, start):
        cols = pl.ds(i // 2 * WIDE, WIDE)
        at = region(s, n, start + (i % 2) * QUART, QUART, cols)
        return send(at, at, dsend.at[i, s], dsem.at[i, s], diag_devs[i])

    def pass_on(s, n, i):
        start, cols = (x_at, 0) if i < 2 else (y_at, WIDE)
        at = region(s, n, start + (i % 2) * QUART, QUART, pl.ds(cols, WIDE))
        dev = (yr_dev, yl_dev, xr_dev, xl_dev)[i]
        return send(at, at, dsend.at[i, s], dsem.at[i, s], dev)

    def to_sibling(s, n):
        at = region(s, n, c * 128, 128)
        return send(at, at, csend.at[s], csem.at[s], sibling)

    w_sibling = send(w_ref, w_sib, wxsend, wxsem, sibling)

    def lt_sibling(s, n):
        lo = max(2 * s - 1, 0) if isinstance(s, int) else jnp.maximum(2 * s - 1, 0)
        return send(
            lt_out.at[pl.ds(lo, n)], lt_ref.at[c, pl.ds(lo, n)], ltsend.at[s], ltsem.at[s], sibling
        )

    def scores(s, n):
        lo = jnp.maximum(2 * s - 1, 0)
        x = f_ref[pl.ds(lo, n), rows(c * 128, 128), :].reshape(n * 128, 2048)
        own, other = (
            lax.dot_general(
                w[...], x, (((1,), (1,)), ((), ())), preferred_element_type=jnp.float32
            )
            for w in (w_ref, w_sib)
        )
        m = jnp.maximum(
            jnp.max(own, axis=0, keepdims=True), jnp.max(other, axis=0, keepdims=True)
        )
        total = jnp.sum(jnp.exp(own - m), axis=0, keepdims=True) + jnp.sum(
            jnp.exp(other - m), axis=0, keepdims=True
        )
        v = m + jnp.log(total)
        for i in range(n):
            cols = slice(i * 128, (i + 1) * 128)
            lt_ref[c, lo + i] = own[:, cols]
            lt_out[lo + i] = other[:, cols]
            msg[pl.ds(lo + i, 1), :] = v[:, cols]
        lt_sibling(s, n).start()

    def each(s, go):
        pair = jnp.logical_and(s > 0, s < 4)
        pl.when(pair)(lambda: go(s, 2))
        pl.when(jnp.logical_not(pair))(lambda: go(s, 1))

    lab_plane = [
        send(lab.at[0], lab_p.at[i], lpsend.at[i], lpsem.at[i], peer)
        for i, peer in enumerate(plane_peers)
    ]
    lab_z = [
        (
            send(lab.at[0], lab.at[SLOT[(-i - 1) % Z]], lzsend.at[i], lzsem.at[i], peer),
            send(lab.at[0], lab.at[SLOT[(-i - 1) % Z]], lzsend.at[i], lzsem.at[i], peer),
        )
        for i, peer in enumerate(z_peers)
    ]
    lab_sibling = send(lab, lab_c, lcsend, lcsem, sibling)

    def step(n, carry):
        @pl.when(n == 1)
        def _():
            w_copy.wait()
            w_sibling.start()

        @pl.when(n == 2)
        def _():
            w_sibling.wait_recv()

        @pl.when(n < 5)
        def _():
            for q in range(PIECES):
                @pl.when(n == 0)
                def _():
                    first_wait(q)
                    to_z(0, 1, q, up_dev).start()
                    to_z(0, 2, q, down_dev).start()

                @pl.when(jnp.logical_and(n > 0, n < 3))
                def _():
                    z_wait(2 * n - 1, q)
                    to_z(2 * n - 1, 2 * n + 1, q, up_dev).start()
                    z_wait(2 * n, q)
                    to_z(2 * n, 2 * n + 2, q, down_dev).start()

                @pl.when(n == 3)
                def _():
                    z_wait(5, q)
                    z_wait(6, q)
                    if q < PIECES // 2:
                        to_z(5, 7, q, up_dev).start()
                    else:
                        to_z(6, 7, q, down_dev).start()

                @pl.when(n == 4)
                def _():
                    z_wait(7, q)

                if q % (PIECES // 2) == PIECES // 2 - 1:
                    side = q // (PIECES // 2)

                    def go(s, m):
                        for i in (side, 2 + side):
                            to_xy(s, m, i, mine_at).start()

                    each(n, go)

        @pl.when(jnp.logical_and(n >= 1, n < 6))
        def _():
            def go(s, m):
                for i in range(4):
                    to_xy(s, m, i, x_at if i < 2 else y_at).wait_recv()
                    pass_on(s, m, i).start()

            each(n - 1, go)

        @pl.when(jnp.logical_and(n >= 2, n < 7))
        def _():
            def go(s, m):
                for i in range(4):
                    to_diag(s, m, i, diag_at).wait_recv()
                to_sibling(s, m).start()

            each(n - 2, go)

        @pl.when(n == 5)
        def _():
            for copy in lab_plane:
                copy.start()

        @pl.when(n >= 4)
        def _():
            def ready(s, carry):
                each(s, scores)
                return carry

            lax.fori_loop(2 * (n - 4), jnp.minimum(2 * (n - 3), 5), ready, 0)

        return carry

    lab_copy.wait()
    other_copy.wait()
    lane = lax.broadcasted_iota(jnp.int32, (2, LANES), 1)
    line = lax.broadcasted_iota(jnp.int32, (2, LANES), 0)
    spot = high * 2 + c
    ids = [jnp.concatenate([lab_ref[:, i * 32 : i * 32 + 32]] * 4, axis=1) for i in range(2)]
    ids = jnp.where(line == 0, ids[0], ids[1]).astype(jnp.float32)
    lab[0] = jnp.where(div(lane, 32) == spot, ids, -1.0)

    lines = [
        jnp.concatenate(
            [other_ref[pl.ds(2 * rem(z + o + Z, Z) + hh, 1), :] for o in OFFSET], axis=0
        )
        for hh in range(2)
    ]
    halves = [
        jnp.concatenate(
            [lines[hh][:, cc * 64 + i * 32 : cc * 64 + i * 32 + 32] for hh in range(2) for cc in range(2)],
            axis=1,
        )
        for i in range(2)
    ]
    other_ref[0:8, :] = jnp.where(c == 0, halves[0], halves[1])

    lax.fori_loop(0, 7, step, 0)

    def exchange(src, dst, ssems, rsems, peers):
        copies = [
            send(src, dst.at[i], ssems.at[i], rsems.at[i], peer) for i, peer in enumerate(peers)
        ]
        for copy in copies:
            copy.start()
        for copy in copies:
            copy.wait()

    for copy in lab_plane:
        copy.wait()
    lab[0] = max_of([lab[0]] + [lab_p[i] for i in range(15)])
    for copy, _ in lab_z:
        copy.start()
    exchange(msg, got_p, psend, psem, plane_peers)
    msg_z[...] = lse_of([msg[...]] + [got_p[i] for i in range(15)])
    exchange(msg_z, got_z, z2send, z2sem, z_peers)
    sums = []
    for j, o in enumerate(OFFSET):
        parts = [msg_z[j : j + 1, :]]
        for i in range(7):
            at = SLOT[(o + i + 1) % Z]
            parts.append(got_z[i, at : at + 1, :])
        sums.append(parts)
    slab = lse_of([jnp.concatenate([p[i] for p in sums], axis=0) for i in range(8)])
    other = other_ref[0:8, :]
    top = jnp.maximum(slab, other)
    fin[c] = top + jnp.log(jnp.exp(slab - top) + jnp.exp(other - top))
    fin_sibling = send(fin.at[c], fin.at[c], c2send, c2sem, sibling)
    fin_sibling.start()
    for copy, arrived in lab_z:
        copy.wait_send()
        arrived.wait_recv()
    lab_sibling.start()
    fin_sibling.wait()
    lab_sibling.wait()
    for s in range(5):
        lt_sibling(s, 2 if 0 < s < 4 else 1).wait()

    def own_part(v):
        part = v[:, 0:32]
        for i in range(1, 4):
            part = jnp.where(spot == i, v[:, i * 32 : i * 32 + 32], part)
        return part

    own_ref[...] = jnp.concatenate([own_part(fin[i, 0:1, :]) for i in range(2)], axis=1)

    base = off_ref[0] + (b * 8 + k) * 512

    def delta(slot, carry):
        ids = jnp.maximum(lab[slot], lab_c[slot]).astype(jnp.int32) - base
        for i in range(2):
            hot = lax.broadcasted_iota(jnp.int32, (512, 128), 0) == ids[i : i + 1, :]
            p = jnp.exp(lt_ref[i, slot] - fin[i, pl.ds(slot, 1), :]) - jnp.where(hot, 1.0, 0.0)
            at = pl.multiple_of(slot * PLANE + i * 128, 128)
            d_ref[:, pl.ds(at, 128)] = p.astype(jnp.bfloat16)
        return carry

    lax.fori_loop(0, 8, delta, 0)
    a_copy.wait()

    w_sibling.wait_send()
    for q in range(PIECES):
        for i in range(2):
            @pl.when(jnp.logical_and(holder, jnp.logical_not(jnp.logical_and(mine, c == i))))
            def _():
                first_to(i, q, sibling).wait_send()
        for slot in range(1, 8):
            to_z(slot, slot, q, up_dev).wait_send()
    for s in range(5):
        m = 2 if 0 < s < 4 else 1
        to_sibling(s, m).wait()
        for i in range(4):
            to_xy(s, m, i, mine_at).wait_send()
            to_diag(s, m, i, mine_at).wait_send()


def gather(offset, features, labels, other, weight, accum):
    dma = pltpu.SemaphoreType.DMA
    hbm = pl.BlockSpec(memory_space=pltpu.HBM)
    vmem = pl.BlockSpec(memory_space=pltpu.VMEM)
    f32 = jnp.float32
    return pl.pallas_call(
        gather_kernel,
        out_shape=(
            jax.ShapeDtypeStruct((8, PLANE, 2048), jnp.bfloat16),
            jax.ShapeDtypeStruct((512, 2048), jnp.bfloat16),
            jax.ShapeDtypeStruct((512, 2048), jnp.bfloat16),
            jax.ShapeDtypeStruct((512, 2048), f32),
            jax.ShapeDtypeStruct((1, 64), f32),
        ),
        in_specs=[pl.BlockSpec(memory_space=pltpu.SMEM)] + [hbm] * 5,
        out_specs=(vmem,) * 5,
        scratch_shapes=[
            pltpu.VMEM((1, 64), jnp.int32),
            pltpu.VMEM((16, LANES), f32),
            pltpu.VMEM((2, 8, 512, 128), f32),
            pltpu.VMEM((8, LANES), f32),
            pltpu.VMEM((15, 8, LANES), f32),
            pltpu.VMEM((8, LANES), f32),
            pltpu.VMEM((7, 8, LANES), f32),
            pltpu.VMEM((2, 8, LANES), f32),
            pltpu.VMEM((8, 2, LANES), f32),
            pltpu.VMEM((15, 2, LANES), f32),
            pltpu.VMEM((8, 2, LANES), f32),
            pltpu.VMEM((64, 2048), jnp.bfloat16),
            pltpu.VMEM((512, 2048), jnp.bfloat16),
            pltpu.VMEM((8, 512, 128), f32),
            dma, dma, dma((3,)), dma((PIECES,)), dma((PIECES,)), dma((2, PIECES)),
            dma((8, PIECES)), dma((8, PIECES)),
            dma((4, 5)), dma((4, 5)), dma((4, 5)), dma((4, 5)), dma((5,)), dma((5,)),
            dma((15,)), dma((15,)), dma((7,)), dma((7,)), dma, dma,
            dma((15,)), dma((15,)), dma((7,)), dma((7,)), dma, dma, dma, dma, dma((5,)), dma((5,)),
        ],
        compiler_params=pltpu.CompilerParams(
            collective_id=0, has_side_effects=True, vmem_limit_bytes=20 << 20
        ),
    )(offset, *(pltpu.with_memory_space_constraint(v, pltpu.HBM) for v in (features, labels, other, weight, accum)))


TILES = ((0, 1024), (1024, 512), (1536, 512))


def update_kernel(
    d_ref, f_ref, w_ref, a_ref, own_ref, nw_hbm, na_hbm, own_hbm, nw_ref, na_ref, sem, osem
):
    own_copy = pltpu.make_async_copy(own_ref, own_hbm, osem)
    own_copy.start()

    def copies(t):
        cols = pl.ds(*TILES[t])
        return (
            pltpu.make_async_copy(nw_ref.at[:, cols], nw_hbm.at[:, cols], sem.at[0, t]),
            pltpu.make_async_copy(na_ref.at[:, cols], na_hbm.at[:, cols], sem.at[1, t]),
        )

    for t, (at, size) in enumerate(TILES):
        cols = pl.ds(at, size)
        grad = jnp.dot(d_ref[...], f_ref[:, cols], preferred_element_type=jnp.float32)
        acc = a_ref[:, cols] + grad * grad
        na_ref[:, cols] = acc
        step = 0.05 * grad / (acc * lax.rsqrt(acc) + 1e-10)
        nw_ref[:, cols] = (w_ref[:, cols].astype(jnp.float32) - step).astype(jnp.bfloat16)
        for copy in copies(t):
            copy.start()
    for t in range(len(TILES)):
        for copy in copies(t):
            copy.wait()
    own_copy.wait()


def update(delta, rows, weight, accum, own):
    vmem = pl.BlockSpec(memory_space=pltpu.VMEM)
    hbm = pl.BlockSpec(memory_space=pltpu.HBM)
    return pl.pallas_call(
        update_kernel,
        out_shape=(
            jax.ShapeDtypeStruct((512, 2048), jnp.bfloat16),
            jax.ShapeDtypeStruct((512, 2048), jnp.float32),
            jax.ShapeDtypeStruct((1, 64), jnp.float32),
        ),
        in_specs=[vmem] * 5,
        out_specs=(hbm,) * 3,
        scratch_shapes=[
            pltpu.VMEM((512, 2048), jnp.bfloat16),
            pltpu.VMEM((512, 2048), jnp.float32),
            pltpu.SemaphoreType.DMA((2, len(TILES))),
            pltpu.SemaphoreType.DMA,
        ],
        compiler_params=pltpu.CompilerParams(vmem_limit_bytes=16 << 20),
    )(delta, rows, weight, accum, own)


def body(features, labels, offset, other_lse, weight, accum):
    rows, delta, w, a, own = gather(
        offset, features, labels.reshape(1, 64), other_lse.reshape(16, LANES), weight, accum
    )
    new_weight, new_accum, own = update(delta, rows.reshape(2048, 2048), w, a, own)
    return (new_weight, new_accum, own.reshape(64))


def solution(mesh):
    in_specs = (
        P("blk", None),
        P("blk"),
        P(),
        P(),
        P(("blk", "cls"), None),
        P(("blk", "cls"), None),
    )
    out_specs = (P(("blk", "cls"), None), P(("blk", "cls"), None), P("blk"))
    return jax.shard_map(body, mesh=mesh, in_specs=in_specs, out_specs=out_specs, check_vma=False)
```

```python
import jax
import jax.numpy as jnp
from jax import lax
from jax.experimental import pallas as pl
from jax.experimental.pallas import tpu as pltpu
from jax.sharding import PartitionSpec as P

MESH = pl.DeviceIdType.MESH
X, Y, Z = 4, 4, 8
HALF, QUART, WIDE = 32, 16, 1024
PLANE = 256
OFFSET = (0, -1, 1, -2, 2, -3, 3, 4)
SLOT = {o % Z: j for j, o in enumerate(OFFSET)}
LANES = 128
PIECES = 4
PIECE = HALF // PIECES


def rem(a, b):
    return lax.rem(a, jnp.int32(b))


def div(a, b):
    return lax.div(a, jnp.int32(b))


def coords():
    b = lax.axis_index("blk")
    k = lax.axis_index("cls")
    z, h, c = div(b, 4), rem(div(b, 2), 2), rem(b, 2)
    x, low = div(k, 2), rem(k, 2)
    return b, k, x, 2 * h + low, z, c


def device(x, y, z, c):
    return (z * 4 + div(y, 2) * 2 + c, x * 2 + rem(y, 2))


def lse_of(parts):
    m = parts[0]
    for v in parts[1:]:
        m = jnp.maximum(m, v)
    s = jnp.exp(parts[0] - m)
    for v in parts[1:]:
        s = s + jnp.exp(v - m)
    return m + jnp.log(s)


def max_of(parts):
    m = parts[0]
    for v in parts[1:]:
        m = jnp.maximum(m, v)
    return m


def gather_kernel(
    off_ref, feat_hbm, lab_hbm, other_hbm, w_hbm, a_hbm,
    f_ref, d_ref, w_ref, a_ref, own_ref,
    lab_ref, other_ref, lt_ref, msg, got_p, msg_z, got_z, fin, lab, lab_p, lab_c, own_f, w_sib, lt_out,
    wsem, asem, osem, lsem, isem, isend, zsem, zsend, xysem, xysend, dsem, dsend, csem, csend,
    psem, psend, z2sem, z2send, c2sem, c2send, lpsem, lpsend, lzsem, lzsend, lcsem, lcsend,
    wxsem, wxsend, ltsem, ltsend,
):
    b, k, x, y, z, c = coords()
    par, low, high = rem(x, 2), rem(y, 2), div(y, 2)
    up, down = rem(z + 1, Z), rem(z + Z - 1, Z)
    xr, xl = rem(x + 1, X), rem(x + X - 1, X)
    yr, yl = rem(y + 1, Y), rem(y + Y - 1, Y)
    sibling = device(x, y, z, 1 - c)
    up_dev, down_dev = device(x, y, up, c), device(x, y, down, c)
    xr_dev, xl_dev = device(xr, y, z, c), device(xl, y, z, c)
    yr_dev, yl_dev = device(x, yr, z, c), device(x, yl, z, c)
    cross = device(x, 3 - y, z, 1 - c)
    diag_devs = [device(i, j, z, c) for j in (yr, yl) for i in (xr, xl)]

    plane_peers = [
        device(rem(x + i // 4, X), rem(y + i % 4, Y), z, c) for i in (10, 6, 14, 9, 11, 2, 8, 5, 7, 13, 15, 1, 3, 4, 12)
    ]
    z_peers = [device(x, y, rem(z + i, Z), c) for i in range(1, 8)]

    f_copy = pltpu.make_async_copy(feat_hbm, own_f, osem.at[2])
    f_copy.start()
    w_copy = pltpu.make_async_copy(w_hbm, w_ref, wsem)
    w_copy.start()
    a_copy = pltpu.make_async_copy(a_hbm, a_ref, asem)
    a_copy.start()
    lab_copy = pltpu.make_async_copy(lab_hbm, lab_ref, osem.at[0])
    lab_copy.start()
    other_copy = pltpu.make_async_copy(other_hbm, other_ref, osem.at[1])
    other_copy.start()

    barrier = pltpu.get_barrier_semaphore()
    near = [xr_dev, xl_dev, yr_dev, yl_dev, up_dev, down_dev, sibling, cross]
    for peer in near:
        pl.semaphore_signal(barrier, inc=1, device_id=peer, device_id_type=MESH)
    pl.semaphore_wait(barrier, len(near))
    f_copy.wait()

    def rows(start, size):
        return pl.ds(pl.multiple_of(start, 8), size)

    def unit(hh, cc):
        return c * 128 + (hh * 2 + cc) * HALF

    mine_at = unit(low, par)
    x_at = unit(low, 1 - par)
    y_at = unit(1 - low, par)
    diag_at = unit(1 - low, 1 - par)

    def send(src, dst, ssem, rsem, dev):
        return pltpu.make_async_remote_copy(
            src_ref=src, dst_ref=dst, send_sem=ssem, recv_sem=rsem,
            device_id=dev, device_id_type=MESH,
        )

    holder = par == c
    mine = low == high

    def first_refs(i, q):
        start = i * 128 + (high * 2 + c) * HALF + q * PIECE
        return (
            own_f.at[pl.ds(i * HALF + q * PIECE, PIECE), :],
            f_ref.at[0, rows(start, PIECE), :],
        )

    def first_to(i, q, dev):
        src, dst = first_refs(i, q)
        return send(src, dst, isend.at[i, q], isem.at[q], dev)

    def first_local(i, q):
        src, dst = first_refs(i, q)
        return pltpu.make_async_copy(src, dst, lsem.at[q])

    local = jnp.logical_and(holder, mine)
    for q in range(PIECES):
        for i in range(2):
            @pl.when(jnp.logical_and(local, c == i))
            def _():
                first_local(i, q).start()

            @pl.when(jnp.logical_and(local, c != i))
            def _():
                first_to(i, q, sibling).start()

            @pl.when(jnp.logical_and(holder, jnp.logical_not(mine)))
            def _():
                first_to(i, q, device(x, 3 - y, z, jnp.int32(i))).start()

    def first_wait(q):
        for i in range(2):
            @pl.when(jnp.logical_and(local, c == i))
            def _():
                first_local(i, q).wait()

        @pl.when(jnp.logical_not(local))
        def _():
            at = f_ref.at[0, rows(mine_at + q * PIECE, PIECE), :]
            send(at, at, isend.at[0, q], isem.at[q], sibling).wait_recv()

    def piece(slot, start, size):
        return f_ref.at[slot, rows(start, size), :]

    def to_z(slot, dst_slot, q, dev):
        start = mine_at + q * PIECE
        return send(
            piece(slot, start, PIECE), piece(dst_slot, start, PIECE),
            zsend.at[dst_slot, q], zsem.at[dst_slot, q], dev,
        )

    def z_wait(slot, q):
        to_z(slot, slot, q, up_dev).wait_recv()

    def region(s, n, start, size, cols=slice(None)):
        lo = max(2 * s - 1, 0) if isinstance(s, int) else jnp.maximum(2 * s - 1, 0)
        return f_ref.at[pl.ds(lo, n), rows(start, size), cols]

    def to_xy(s, n, i, start):
        at = region(s, n, start + (i % 2) * QUART, QUART)
        dev = (xr_dev, xl_dev, yr_dev, yl_dev)[i]
        return send(at, at, xysend.at[i, s], xysem.at[i, s], dev)

    def to_diag(s, n, i, start):
        cols = pl.ds(i // 2 * WIDE, WIDE)
        at = region(s, n, start + (i % 2) * QUART, QUART, cols)
        return send(at, at, dsend.at[i, s], dsem.at[i, s], diag_devs[i])

    def pass_on(s, n, i):
        start, cols = (x_at, 0) if i < 2 else (y_at, WIDE)
        at = region(s, n, start + (i % 2) * QUART, QUART, pl.ds(cols, WIDE))
        dev = (yr_dev, yl_dev, xr_dev, xl_dev)[i]
        return send(at, at, dsend.at[i, s], dsem.at[i, s], dev)

    def to_sibling(s, n):
        at = region(s, n, c * 128, 128)
        return send(at, at, csend.at[s], csem.at[s], sibling)

    w_sibling = send(w_ref, w_sib, wxsend, wxsem, sibling)

    def lt_sibling(s, n):
        lo = max(2 * s - 1, 0) if isinstance(s, int) else jnp.maximum(2 * s - 1, 0)
        return send(
            lt_out.at[pl.ds(lo, n)], lt_ref.at[c, pl.ds(lo, n)], ltsend.at[s], ltsem.at[s], sibling
        )

    def scores(s, n):
        lo = jnp.maximum(2 * s - 1, 0)
        x = f_ref[pl.ds(lo, n), rows(c * 128, 128), :].reshape(n * 128, 2048)
        own, other = (
            lax.dot_general(
                w[...], x, (((1,), (1,)), ((), ())), preferred_element_type=jnp.float32
            )
            for w in (w_ref, w_sib)
        )
        m = jnp.maximum(
            jnp.max(own, axis=0, keepdims=True), jnp.max(other, axis=0, keepdims=True)
        )
        total = jnp.sum(jnp.exp(own - m), axis=0, keepdims=True) + jnp.sum(
            jnp.exp(other - m), axis=0, keepdims=True
        )
        v = m + jnp.log(total)
        for i in range(n):
            cols = slice(i * 128, (i + 1) * 128)
            lt_ref[c, lo + i] = own[:, cols]
            lt_out[lo + i] = other[:, cols]
            msg[pl.ds(lo + i, 1), :] = v[:, cols]
        lt_sibling(s, n).start()

    def each(s, go):
        pair = jnp.logical_and(s > 0, s < 4)
        pl.when(pair)(lambda: go(s, 2))
        pl.when(jnp.logical_not(pair))(lambda: go(s, 1))

    lab_plane = [
        send(lab.at[0], lab_p.at[i], lpsend.at[i], lpsem.at[i], peer)
        for i, peer in enumerate(plane_peers)
    ]
    lab_z = [
        (
            send(lab.at[0], lab.at[SLOT[(-i - 1) % Z]], lzsend.at[i], lzsem.at[i], peer),
            send(lab.at[0], lab.at[SLOT[(-i - 1) % Z]], lzsend.at[i], lzsem.at[i], peer),
        )
        for i, peer in enumerate(z_peers)
    ]
    lab_sibling = send(lab, lab_c, lcsend, lcsem, sibling)

    def step(n, carry):
        @pl.when(n == 1)
        def _():
            w_copy.wait()
            w_sibling.start()

        @pl.when(n == 2)
        def _():
            w_sibling.wait_recv()

        @pl.when(n < 5)
        def _():
            for q in range(PIECES):
                @pl.when(n == 0)
                def _():
                    first_wait(q)
                    to_z(0, 1, q, up_dev).start()
                    to_z(0, 2, q, down_dev).start()

                @pl.when(jnp.logical_and(n > 0, n < 3))
                def _():
                    z_wait(2 * n - 1, q)
                    to_z(2 * n - 1, 2 * n + 1, q, up_dev).start()
                    z_wait(2 * n, q)
                    to_z(2 * n, 2 * n + 2, q, down_dev).start()

                @pl.when(n == 3)
                def _():
                    z_wait(5, q)
                    z_wait(6, q)
                    if q < PIECES // 2:
                        to_z(5, 7, q, up_dev).start()
                    else:
                        to_z(6, 7, q, down_dev).start()

                @pl.when(n == 4)
                def _():
                    z_wait(7, q)

                if q % (PIECES // 2) == PIECES // 2 - 1:
                    side = q // (PIECES // 2)

                    def go(s, m):
                        for i in (side, 2 + side):
                            to_xy(s, m, i, mine_at).start()

                    each(n, go)

        @pl.when(jnp.logical_and(n >= 1, n < 6))
        def _():
            def go(s, m):
                for i in range(4):
                    to_xy(s, m, i, x_at if i < 2 else y_at).wait_recv()
                    pass_on(s, m, i).start()

            each(n - 1, go)

        @pl.when(jnp.logical_and(n >= 2, n < 7))
        def _():
            def go(s, m):
                for i in range(4):
                    to_diag(s, m, i, diag_at).wait_recv()
                to_sibling(s, m).start()

            each(n - 2, go)

        @pl.when(n == 5)
        def _():
            for copy in lab_plane:
                copy.start()

        @pl.when(n >= 4)
        def _():
            def ready(s, carry):
                each(s, scores)
                return carry

            lax.fori_loop(2 * (n - 4), jnp.minimum(2 * (n - 3), 5), ready, 0)

        return carry

    lab_copy.wait()
    other_copy.wait()
    lane = lax.broadcasted_iota(jnp.int32, (2, LANES), 1)
    line = lax.broadcasted_iota(jnp.int32, (2, LANES), 0)
    spot = high * 2 + c
    ids = [jnp.concatenate([lab_ref[:, i * 32 : i * 32 + 32]] * 4, axis=1) for i in range(2)]
    ids = jnp.where(line == 0, ids[0], ids[1]).astype(jnp.float32)
    lab[0] = jnp.where(div(lane, 32) == spot, ids, -1.0)

    lines = [
        jnp.concatenate(
            [other_ref[pl.ds(2 * rem(z + o + Z, Z) + hh, 1), :] for o in OFFSET], axis=0
        )
        for hh in range(2)
    ]
    halves = [
        jnp.concatenate(
            [lines[hh][:, cc * 64 + i * 32 : cc * 64 + i * 32 + 32] for hh in range(2) for cc in range(2)],
            axis=1,
        )
        for i in range(2)
    ]
    other_ref[0:8, :] = jnp.where(c == 0, halves[0], halves[1])

    lax.fori_loop(0, 7, step, 0)

    def exchange(src, dst, ssems, rsems, peers):
        copies = [
            send(src, dst.at[i], ssems.at[i], rsems.at[i], peer) for i, peer in enumerate(peers)
        ]
        for copy in copies:
            copy.start()
        for copy in copies:
            copy.wait()

    for copy in lab_plane:
        copy.wait()
    lab[0] = max_of([lab[0]] + [lab_p[i] for i in range(15)])
    for copy, _ in lab_z:
        copy.start()
    exchange(msg, got_p, psend, psem, plane_peers)
    msg_z[...] = lse_of([msg[...]] + [got_p[i] for i in range(15)])
    exchange(msg_z, got_z, z2send, z2sem, z_peers)
    sums = []
    for j, o in enumerate(OFFSET):
        parts = [msg_z[j : j + 1, :]]
        for i in range(7):
            at = SLOT[(o + i + 1) % Z]
            parts.append(got_z[i, at : at + 1, :])
        sums.append(parts)
    slab = lse_of([jnp.concatenate([p[i] for p in sums], axis=0) for i in range(8)])
    other = other_ref[0:8, :]
    top = jnp.maximum(slab, other)
    fin[c] = top + jnp.log(jnp.exp(slab - top) + jnp.exp(other - top))
    fin_sibling = send(fin.at[c], fin.at[c], c2send, c2sem, sibling)
    fin_sibling.start()
    for copy, arrived in lab_z:
        copy.wait_send()
        arrived.wait_recv()
    lab_sibling.start()
    fin_sibling.wait()
    lab_sibling.wait()
    for s in range(5):
        lt_sibling(s, 2 if 0 < s < 4 else 1).wait()

    def own_part(v):
        part = v[:, 0:32]
        for i in range(1, 4):
            part = jnp.where(spot == i, v[:, i * 32 : i * 32 + 32], part)
        return part

    own_ref[...] = jnp.concatenate([own_part(fin[i, 0:1, :]) for i in range(2)], axis=1)

    base = off_ref[0] + (b * 8 + k) * 512

    def delta(slot, carry):
        ids = jnp.maximum(lab[slot], lab_c[slot]).astype(jnp.int32) - base
        for i in range(2):
            hot = lax.broadcasted_iota(jnp.int32, (512, 128), 0) == ids[i : i + 1, :]
            p = jnp.exp(lt_ref[i, slot] - fin[i, pl.ds(slot, 1), :]) - jnp.where(hot, 1.0, 0.0)
            at = pl.multiple_of(slot * PLANE + i * 128, 128)
            d_ref[:, pl.ds(at, 128)] = p.astype(jnp.bfloat16)
        return carry

    lax.fori_loop(0, 8, delta, 0)
    a_copy.wait()

    w_sibling.wait_send()
    for q in range(PIECES):
        for i in range(2):
            @pl.when(jnp.logical_and(holder, jnp.logical_not(jnp.logical_and(mine, c == i))))
            def _():
                first_to(i, q, sibling).wait_send()
        for slot in range(1, 8):
            to_z(slot, slot, q, up_dev).wait_send()
    for s in range(5):
        m = 2 if 0 < s < 4 else 1
        to_sibling(s, m).wait()
        for i in range(4):
            to_xy(s, m, i, mine_at).wait_send()
            to_diag(s, m, i, mine_at).wait_send()


def gather(offset, features, labels, other, weight, accum):
    dma = pltpu.SemaphoreType.DMA
    hbm = pl.BlockSpec(memory_space=pltpu.HBM)
    vmem = pl.BlockSpec(memory_space=pltpu.VMEM)
    f32 = jnp.float32
    return pl.pallas_call(
        gather_kernel,
        out_shape=(
            jax.ShapeDtypeStruct((8, PLANE, 2048), jnp.bfloat16),
            jax.ShapeDtypeStruct((512, 2048), jnp.bfloat16),
            jax.ShapeDtypeStruct((512, 2048), jnp.bfloat16),
            jax.ShapeDtypeStruct((512, 2048), f32),
            jax.ShapeDtypeStruct((1, 64), f32),
        ),
        in_specs=[pl.BlockSpec(memory_space=pltpu.SMEM)] + [hbm] * 5,
        out_specs=(vmem,) * 5,
        scratch_shapes=[
            pltpu.VMEM((1, 64), jnp.int32),
            pltpu.VMEM((16, LANES), f32),
            pltpu.VMEM((2, 8, 512, 128), f32),
            pltpu.VMEM((8, LANES), f32),
            pltpu.VMEM((15, 8, LANES), f32),
            pltpu.VMEM((8, LANES), f32),
            pltpu.VMEM((7, 8, LANES), f32),
            pltpu.VMEM((2, 8, LANES), f32),
            pltpu.VMEM((8, 2, LANES), f32),
            pltpu.VMEM((15, 2, LANES), f32),
            pltpu.VMEM((8, 2, LANES), f32),
            pltpu.VMEM((64, 2048), jnp.bfloat16),
            pltpu.VMEM((512, 2048), jnp.bfloat16),
            pltpu.VMEM((8, 512, 128), f32),
            dma, dma, dma((3,)), dma((PIECES,)), dma((PIECES,)), dma((2, PIECES)),
            dma((8, PIECES)), dma((8, PIECES)),
            dma((4, 5)), dma((4, 5)), dma((4, 5)), dma((4, 5)), dma((5,)), dma((5,)),
            dma((15,)), dma((15,)), dma((7,)), dma((7,)), dma, dma,
            dma((15,)), dma((15,)), dma((7,)), dma((7,)), dma, dma, dma, dma, dma((5,)), dma((5,)),
        ],
        compiler_params=pltpu.CompilerParams(
            collective_id=0, has_side_effects=True, vmem_limit_bytes=20 << 20
        ),
    )(offset, *(pltpu.with_memory_space_constraint(v, pltpu.HBM) for v in (features, labels, other, weight, accum)))


TILES = ((0, 1024), (1024, 512), (1536, 512))


def update_kernel(
    d_ref, f_ref, w_ref, a_ref, own_ref, nw_hbm, na_hbm, own_hbm, nw_ref, na_ref, sem, osem
):
    own_copy = pltpu.make_async_copy(own_ref, own_hbm, osem)
    own_copy.start()

    def copies(t):
        cols = pl.ds(*TILES[t])
        return (
            pltpu.make_async_copy(nw_ref.at[:, cols], nw_hbm.at[:, cols], sem.at[0, t]),
            pltpu.make_async_copy(na_ref.at[:, cols], na_hbm.at[:, cols], sem.at[1, t]),
        )

    for t, (at, size) in enumerate(TILES):
        cols = pl.ds(at, size)
        grad = jnp.dot(d_ref[...], f_ref[:, cols], preferred_element_type=jnp.float32)
        acc = a_ref[:, cols] + grad * grad
        na_ref[:, cols] = acc
        step = 0.05 * grad / (acc * lax.rsqrt(acc) + 1e-10)
        nw_ref[:, cols] = (w_ref[:, cols].astype(jnp.float32) - step).astype(jnp.bfloat16)
        for copy in copies(t):
            copy.start()
    for t in range(len(TILES)):
        for copy in copies(t):
            copy.wait()
    own_copy.wait()


def update(delta, rows, weight, accum, own):
    vmem = pl.BlockSpec(memory_space=pltpu.VMEM)
    hbm = pl.BlockSpec(memory_space=pltpu.HBM)
    return pl.pallas_call(
        update_kernel,
        out_shape=(
            jax.ShapeDtypeStruct((512, 2048), jnp.bfloat16),
            jax.ShapeDtypeStruct((512, 2048), jnp.float32),
            jax.ShapeDtypeStruct((1, 64), jnp.float32),
        ),
        in_specs=[vmem] * 5,
        out_specs=(hbm,) * 3,
        scratch_shapes=[
            pltpu.VMEM((512, 2048), jnp.bfloat16),
            pltpu.VMEM((512, 2048), jnp.float32),
            pltpu.SemaphoreType.DMA((2, len(TILES))),
            pltpu.SemaphoreType.DMA,
        ],
        compiler_params=pltpu.CompilerParams(vmem_limit_bytes=16 << 20),
    )(delta, rows, weight, accum, own)


def body(features, labels, offset, other_lse, weight, accum):
    rows, delta, w, a, own = gather(
        offset, features, labels.reshape(1, 64), other_lse.reshape(16, LANES), weight, accum
    )
    new_weight, new_accum, own = update(delta, rows.reshape(2048, 2048), w, a, own)
    return (new_weight, new_accum, own.reshape(64))


def solution(mesh):
    in_specs = (
        P("blk", None),
        P("blk"),
        P(),
        P(),
        P(("blk", "cls"), None),
        P(("blk", "cls"), None),
    )
    out_specs = (P(("blk", "cls"), None), P(("blk", "cls"), None), P("blk"))
    return jax.shard_map(body, mesh=mesh, in_specs=in_specs, out_specs=out_specs, check_vma=False)
```
